128 devices in a mesh: seq: 16 (over y, x), chan: 8 (over z, core).
Axes of the slice: x: 4, y: 4, z: 4, core: 2. Of those that a mesh axis runs over, the one named last changes fastest.
Arguments:
- signal: bfloat16 [256, 32768], P('chan', 'seq'), may hold values from -6 to 6
- gate_values: bfloat16 [256, 32768], P('chan', 'seq'), may hold values from -6 to 6
- filter_taps: float32 [256, 32768], P('chan', 'seq'), may hold values from -6 to 6
- skip_gain: float32 [256], P('chan'), may hold values from 0.5 to 1.5
- positive: bfloat16 [256, 32768], P('chan', 'seq'), may hold values from -6 to 6
- item_table: bfloat16 [256, 524288], P('chan', 'seq'), may hold values from -6 to 6
- item_row: int32 [524288], replicated, may hold values from 0 to 524287, as said below
- negative_ids: int32 [256, 64], P('seq'), may hold values from 0 to 524287, as said below
- block_counts: int32 [256], P('seq'), may hold values from 1 to 64, 10240 in all
Outputs:
- grad_signal: float32 [256, 32768], P('chan', 'seq')
- grad_gate: bfloat16 [256, 32768], P('chan', 'seq')
- grad_filter: float32 [256, 32768], P('chan', 'seq')
- grad_table: float32 [256, 524288], P('chan', 'seq')
The draws below stay inside these ranges and needn't reach their ends.
Inputs may be any that keep to these rules, and one draw needn't show every extreme that they name: `item_row`: A permutation of the item ids. `negative_ids`: of the 1024 ids in the blocks of one index of seq, at most 96 map under item_row to rows of one owner (row // 32768); one owner receives exactly 96 from every index of seq, and for every index some owner receives exactly 96. `block_counts`: the valid negatives of a block are the first ones of its row of negative_ids.
All inputs are finite; a program needn't handle non-finite values.
Results may differ from the reference program's by a relative error of at most 0.015.
Values may be sent and summed in bfloat16 or wider, within the bound.
A program may use at most 128 MiB of HBM per device.

```python
import math
import jax
import jax.numpy as jnp
import numpy as np

C = 256
BLK = 128
NNEG = 64
ROWS_OWN = 32768
SEQ_LEN = 32768
ITEMS = 524288
NBLOCKS = 256
SLOTS = 1024
OWNERS = 16
CAP = 96


def shared_tables(key):
    ordering = jax.random.permutation(jax.random.fold_in(key, 5), ITEMS).astype(jnp.int32)
    inverse = jnp.zeros((ITEMS,), jnp.int32).at[ordering].set(jnp.arange(ITEMS, dtype=jnp.int32))
    return (ordering, inverse)


def owner_rows(key):
    entries = OWNERS * CAP
    pool_owner = jnp.arange(entries, dtype=jnp.int32) // CAP
    common = jax.random.randint(jax.random.fold_in(key, 11), (), 0, OWNERS)
    own_pick = jax.random.randint(jax.random.fold_in(key, 12), (OWNERS, 1), 0, OWNERS)
    noise_bits = jax.random.randint(jax.random.fold_in(key, 13), (OWNERS, entries), 0, 1 << 16)
    ranking = noise_bits * entries + jnp.arange(entries, dtype=jnp.int32)[None, :]
    forced = (pool_owner[None, :] == common) | (pool_owner[None, :] == own_pick)
    ranking = jnp.where(forced, ranking - (1 << 30), ranking)
    chosen = jnp.argsort(ranking, axis=1)[:, :SLOTS].astype(jnp.int32) // CAP
    mixing = jax.random.randint(jax.random.fold_in(key, 14), (OWNERS, SLOTS), 0, 1 << 16) * SLOTS
    mixing = mixing + jnp.arange(SLOTS, dtype=jnp.int32)[None, :]
    chosen = jnp.take_along_axis(chosen, jnp.argsort(mixing, axis=1).astype(jnp.int32), axis=1)
    local_row = jax.random.randint(jax.random.fold_in(key, 15), (OWNERS, SLOTS), 0, ROWS_OWN)
    return (chosen * ROWS_OWN + local_row).reshape(NBLOCKS, NNEG)


def draw_item_row(key, part):
    return shared_tables(key)[0]


def draw_negative_ids(key, part):
    inverse = shared_tables(key)[1]
    return inverse[owner_rows(key)]


def block_levels(key, extent, shards, low, top_value):
    factor_of, own = 1.0, jax.random.fold_in(key, 6)
    for position, blocks in shards:
        heights = jnp.exp(jax.random.uniform(jax.random.fold_in(own, position), (blocks,), jnp.float32, low / len(shards), top_value / len(shards)))
        factor_of = factor_of * jnp.repeat(heights, extent[position] // blocks).reshape([-1 if axis == position else 1 for axis in range(len(extent))])
    return factor_of


def profile(amount, total, most, skew):
    weights = [(1 << 20) // math.isqrt(rank ** skew) + 1 for rank in range(2, amount + 1)]
    surplus, given = total - most - (amount - 1), [1] * (amount - 1)
    while surplus > 0:
        free = [i for i in range(amount - 1) if given[i] < most]
        mass, remaining = sum([weights[i] for i in free]), surplus
        for i in free:
            more = min(most - given[i], max(1, remaining * weights[i] // mass), surplus)
            given[i] = given[i] + more
            surplus = surplus - more
    return np.array([most] + given)


def uneven(key, amount, total, limit, skew):
    if amount == 2:
        one = jax.random.randint(key, (), max(1, total - limit), min(limit, total - 1) + 1)
        return jnp.stack([one, total - one])
    sizes = jnp.asarray(profile(amount, total, limit, skew), jnp.int32)
    twos = (amount - 1) // 2
    donor, sink = sizes[1:1 + 2 * twos:2], sizes[2:2 + 2 * twos:2]
    slack = jnp.minimum(donor - 1, limit - sink)
    moved = jax.random.randint(jax.random.fold_in(key, 1), (twos,), 0, 1 << 20) % (slack + 1)
    sizes = sizes.at[1:1 + 2 * twos:2].set(donor - moved).at[2:2 + 2 * twos:2].set(sink + moved)
    return sizes[jax.random.permutation(jax.random.fold_in(key, 2), amount)]


def noise(rng, dims, scale, reach, pieces=(), kind=jnp.bfloat16):
    loudness = block_levels(rng, dims, pieces, -0.22, 0.18) if pieces else 1.0
    values = jax.random.normal(rng, dims, jnp.float32) * scale * loudness
    return jnp.minimum(jnp.maximum(values, -reach), reach).astype(kind)


def setup_inputs(seed: int = 0) -> dict:
    seeds = jax.random.split(jax.random.key(seed), 10)
    signal = noise(seeds[0], (C, SEQ_LEN), 1.0, 6.0, ((0, 8), (1, 16)))
    gate_values = noise(seeds[1], (C, SEQ_LEN), 1.0, 6.0, ((0, 8), (1, 16)))
    filter_taps = noise(seeds[2], (C, SEQ_LEN), 1.0, 6.0, ((0, 8), (1, 16)), jnp.float32)
    skip_gain = jnp.clip(0.5 + 1.0 * jax.random.uniform(seeds[3], (C,), jnp.float32) ** block_levels(seeds[3], (C,), ((0, 8),), -0.2, 0.2), 0.5, 1.5)
    positive = noise(seeds[4], (C, SEQ_LEN), 1.0, 6.0, ((0, 8), (1, 16)))
    item_table = noise(seeds[5], (C, ITEMS), 1.0, 6.0, ((0, 8), (1, 16)))
    item_row = draw_item_row(jax.random.fold_in(seeds[9], 71), 0)
    negative_ids = draw_negative_ids(jax.random.fold_in(seeds[9], 71), 0)
    block_counts = uneven(seeds[8], NBLOCKS, NBLOCKS * NNEG * 5 // 8, NNEG, 2).astype(jnp.int32)
    return dict(signal=signal, gate_values=gate_values, filter_taps=filter_taps, skip_gain=skip_gain, positive=positive, item_table=item_table, item_row=item_row, negative_ids=negative_ids, block_counts=block_counts)


def causal(former, latter):
    length_all = 2 * SEQ_LEN
    spectra = jnp.fft.rfft(former, n=length_all, axis=1) * jnp.fft.rfft(latter, n=length_all, axis=1)
    return jnp.fft.irfft(spectra, n=length_all, axis=1)[:, :SEQ_LEN].astype(jnp.float32)


def lagged(former, latter):
    length_all = 2 * SEQ_LEN
    spectra = jnp.conj(jnp.fft.rfft(former, n=length_all, axis=1)) * jnp.fft.rfft(latter, n=length_all, axis=1)
    return jnp.fft.irfft(spectra, n=length_all, axis=1)[:, :SEQ_LEN].astype(jnp.float32)


def reference(signal, gate_values, filter_taps, skip_gain, positive, item_table, item_row, negative_ids, block_counts):
    filter_scale = SEQ_LEN ** -0.5
    score_scale = C ** -0.5
    source = signal.astype(jnp.float32)
    gating = gate_values.astype(jnp.float32)
    convolved = filter_scale * causal(filter_taps, source)
    pre_gate = convolved + skip_gain[:, None] * source
    encoded = (gating * pre_gate).astype(jnp.bfloat16)
    neg_rows = item_row[negative_ids]
    neg_embed = jnp.transpose(item_table[:, neg_rows], (1, 2, 0)).astype(jnp.float32)
    enc_blocks = encoded.astype(jnp.float32).reshape(C, NBLOCKS, BLK)
    score_neg = score_scale * jnp.einsum("bjc,cbt->btj", neg_embed, enc_blocks)
    score_pos = score_scale * jnp.sum(encoded.astype(jnp.float32) * positive.astype(jnp.float32), axis=0)
    is_valid = jnp.arange(NNEG, dtype=jnp.int32)[None, None, :] < block_counts[:, None, None]
    neg_weight = jnp.where(is_valid, jax.nn.sigmoid(score_neg), 0.0).astype(jnp.bfloat16)
    pos_weight = -jax.nn.sigmoid(-score_pos)
    weights = neg_weight.astype(jnp.float32)
    from_negs = jnp.einsum("btj,bjc->cbt", weights, neg_embed).reshape(C, SEQ_LEN)
    enc_grad = score_scale * (pos_weight[None, :] * positive.astype(jnp.float32) + from_negs)
    slot_grad = score_scale * jnp.einsum("btj,cbt->cbj", weights, enc_blocks).reshape(C, NBLOCKS * NNEG)
    grad_table = jnp.zeros((C, ITEMS), jnp.float32).at[:, neg_rows.reshape(-1)].add(slot_grad)
    grad_gate = (enc_grad * pre_gate).astype(jnp.bfloat16)
    gate_back = enc_grad * gating
    grad_signal = filter_scale * lagged(filter_taps, gate_back) + skip_gain[:, None] * gate_back
    grad_filter = filter_scale * lagged(source, gate_back)
    return grad_signal, grad_gate, grad_filter, grad_table
```

```python
import functools

import jax
import jax.numpy as jnp
import ml_dtypes
import numpy as np
from jax import lax
from jax.experimental import pallas as pl
from jax.experimental.pallas import tpu as pltpu
from jax.sharding import PartitionSpec as P

C = 256
F32, BF16, I32 = jnp.float32, jnp.bfloat16, jnp.int32
VMEM = pl.BlockSpec(memory_space=pltpu.VMEM)
SMEM = pl.BlockSpec(memory_space=pltpu.SMEM)
N1, N2 = 256, 128
LIMIT = 56 * 1024 * 1024
NT = (((1,), (1,)), ((), ()))
TN = (((0,), (0,)), ((), ()))


def halves(matrix):
    high = matrix.astype(ml_dtypes.bfloat16)
    return high, (matrix - high.astype(np.float64)).astype(ml_dtypes.bfloat16)


def transform_tables():
    total = N1 * N2
    k1, n1 = np.arange(N1) + 0.25, np.arange(N1)
    n2 = np.arange(N2)
    first = np.exp(-2j * np.pi * np.outer(k1, n1) / N1)
    turn = np.exp(-2j * np.pi * np.outer(k1, n2) / total)
    last = np.exp(-2j * np.pi * np.outer(n2, n2) / N2)
    fwd1 = np.concatenate(halves(np.concatenate([first.real, first.imag])), axis=1)
    fwd2 = np.block([[last.real, last.imag], [-last.imag, last.real]])
    inv2 = np.block([[last.real, -last.imag], [last.imag, last.real]])
    inv1 = np.concatenate([first.real.T, first.imag.T], axis=1) / total

    def stack_k(matrix):
        high, low = halves(matrix)
        return np.concatenate([high, high, low])

    high, low = halves(inv1)
    inv1 = np.concatenate([high, high, low], axis=1)
    turns = np.concatenate([turn.real, turn.imag], axis=1).astype(np.float32)
    return fwd1, stack_k(fwd2), stack_k(inv2), inv1, turns


def dot(left, right, dims=None):
    if dims is None:
        return jnp.dot(left, right, preferred_element_type=F32)
    return lax.dot_general(left, right, dims, preferred_element_type=F32)


def split(value):
    high = value.astype(BF16)
    return high, (value - high.astype(F32)).astype(BF16)


def spectrum(columns, fwd1, fwd2, turn_r, turn_i):
    joined = jnp.concatenate(columns, axis=1)
    stage = dot(fwd1, jnp.concatenate([joined, joined], axis=0))
    rows = []
    for item in range(len(columns)):
        real = stage[:N1, N2 * item : N2 * (item + 1)]
        imag = stage[N1:, N2 * item : N2 * (item + 1)]
        turned = jnp.concatenate(
            [real * turn_r - imag * turn_i, real * turn_i + imag * turn_r], axis=1
        )
        high, low = split(turned)
        rows.append(jnp.concatenate([high, low, high], axis=1))
    done = dot(jnp.concatenate(rows, axis=0), fwd2)
    return [
        (done[N1 * i : N1 * (i + 1), :N2], done[N1 * i : N1 * (i + 1), N2:])
        for i in range(len(columns))
    ]


def positions(spectra, inv2, inv1, turn_r, turn_i):
    rows = []
    for real, imag in spectra:
        high, low = split(jnp.concatenate([real, imag], axis=1))
        rows.append(jnp.concatenate([high, low, high], axis=1))
    stage = dot(jnp.concatenate(rows, axis=0), inv2)
    columns = []
    for item in range(len(spectra)):
        real = stage[N1 * item : N1 * (item + 1), :N2]
        imag = stage[N1 * item : N1 * (item + 1), N2:]
        columns.append(
            jnp.concatenate(
                [real * turn_r + imag * turn_i, imag * turn_r - real * turn_i], axis=0
            )
        )
    high, low = split(jnp.concatenate(columns, axis=1))
    done = dot(inv1, jnp.concatenate([high, low, high], axis=0))
    return [done[:, N2 * i : N2 * (i + 1)] for i in range(len(spectra))]


def exchange_body(axis, size, count, *refs):
    sources, targets = refs[:count], refs[count : 2 * count]
    send_sem, recv_sem, own_sem = refs[2 * count :]
    me = lax.axis_index(axis)
    barrier = pltpu.get_barrier_semaphore()
    for step in range(1, size):
        pl.semaphore_signal(
            barrier,
            inc=1,
            device_id={axis: lax.rem(me + step, size)},
            device_id_type=pl.DeviceIdType.MESH,
        )
    own = [
        pltpu.make_async_copy(s.at[me], t.at[me], own_sem.at[i])
        for i, (s, t) in enumerate(zip(sources, targets))
    ]
    for copy in own:
        copy.start()
    pl.semaphore_wait(barrier, size - 1)
    copies = []
    for step in range(1, size):
        peer = lax.rem(me + step, size)
        for i, (s, t) in enumerate(zip(sources, targets)):
            copies.append(
                pltpu.make_async_remote_copy(
                    src_ref=s.at[peer],
                    dst_ref=t.at[me],
                    send_sem=send_sem.at[i, step],
                    recv_sem=recv_sem.at[i, step],
                    device_id={axis: peer},
                    device_id_type=pl.DeviceIdType.MESH,
                )
            )
            copies[-1].start()
    for copy in own:
        copy.wait()
    for copy in copies:
        copy.wait()


def exchange(arrays, axis, size, collective_id):
    count = len(arrays)
    return pl.pallas_call(
        functools.partial(exchange_body, axis, size, count),
        out_shape=[jax.ShapeDtypeStruct(a.shape, a.dtype) for a in arrays],
        in_specs=[VMEM] * count,
        out_specs=[VMEM] * count,
        scratch_shapes=[
            pltpu.SemaphoreType.DMA((count, size)),
            pltpu.SemaphoreType.DMA((count, size)),
            pltpu.SemaphoreType.DMA((count,)),
        ],
        compiler_params=pltpu.CompilerParams(
            collective_id=collective_id, has_side_effects=True, vmem_limit_bytes=LIMIT
        ),
        name=f"exchange_{collective_id}",
    )(*arrays)


def call(body, outs, scratch=(), specs=None, name=None):
    def run(*args):
        return pl.pallas_call(
            body,
            out_shape=[jax.ShapeDtypeStruct(s, d) for s, d in outs],
            in_specs=specs or [VMEM] * len(args),
            out_specs=[VMEM] * len(outs),
            scratch_shapes=list(scratch),
            compiler_params=pltpu.CompilerParams(vmem_limit_bytes=LIMIT),
            name=name,
        )(*args)

    return run


def to_rows(value, scratch):
    channels, length = value.shape
    units = length // 128
    for u in range(units):
        scratch[pl.ds(u, channels, stride=units), :] = value[:, 128 * u : 128 * (u + 1)]
    return scratch[...]


def prep_body(rows_ref, signal_ref, taps_ref, data_ref, ask_ref, place_ref, scratch):
    parts, kinds, own, units, width = data_ref.shape
    for kind, ref in enumerate((signal_ref, taps_ref)):
        flat = to_rows(ref[...].astype(F32), scratch).astype(BF16)
        data_ref[:, kind] = flat.reshape(parts, own, units, width)
    rows = rows_ref[...]
    groups = rows.shape[0]
    owner = rows >> 15
    high = ((rows >> 8) & 127).astype(F32)
    low = (rows & 255).astype(F32) + 1.0
    each = lax.broadcasted_iota(I32, (parts, 128), 0)
    onehots = [(owner[b : b + 1, :] == each).astype(F32) for b in range(groups)]
    stacked = jnp.concatenate(onehots, axis=0).astype(BF16)
    size = groups * parts
    above = lax.broadcasted_iota(I32, (128, 128), 0) < lax.broadcasted_iota(I32, (128, 128), 1)
    within = dot(stacked, above.astype(BF16))
    totals = dot(stacked, jnp.ones((128, 128), BF16))
    to, of = lax.broadcasted_iota(I32, (size, size), 0), lax.broadcasted_iota(I32, (size, size), 1)
    earlier = ((to - of) > 0) & (lax.rem(to + size - of, parts) == 0)
    rank = within + dot(earlier.astype(BF16), totals.astype(BF16))
    target = lax.broadcasted_iota(I32, (128, 128), 0).astype(F32)
    asked = jnp.zeros((2 * parts, 128), F32)
    for b in range(groups):
        mine = jnp.sum(onehots[b] * rank[parts * b : parts * (b + 1)], axis=0, keepdims=True)
        place_ref[b : b + 1, :] = owner[b : b + 1, :] * 128 + mine.astype(I32)
        ranks = (target == mine).astype(BF16)
        values = jnp.concatenate(
            [onehots[b] * high[b : b + 1, :], onehots[b] * low[b : b + 1, :]], axis=0
        )
        asked = asked + dot(values.astype(BF16), ranks, NT)
    asked = 256.0 * asked[:parts] + asked[parts:]
    for o in range(parts):
        ask_ref[o] = jnp.broadcast_to(asked[o : o + 1, :], (8, 128))


def lists(ask_ref):
    parts = ask_ref.shape[0]
    row = jnp.concatenate([ask_ref[s][0:1, :] for s in range(parts)], axis=1)
    row = row.astype(I32) - 1
    return row >> 8, row & 255


def forward_body(
    data_ref, ask_ref, table_ref, fwd1, fwd2, inv2, inv1, turns,
    conv_ref, found_ref, spec_ref, folded, picked,
):
    parts, kinds, own, units, width = data_ref.shape
    turn_r, turn_i = turns[:, :N2], turns[:, N2:]
    columns = [
        data_ref[:, kind, c].reshape(N1, N2) for kind in range(kinds) for c in range(own)
    ]
    spectra = spectrum(columns, fwd1[...], fwd2[...], turn_r, turn_i)
    for i, (real, imag) in enumerate(spectra):
        spec_ref[i, 0] = real
        spec_ref[i, 1] = imag
    products = []
    for c in range(own):
        (xr, xi), (hr, hi) = spectra[c], spectra[own + c]
        products.append((xr * hr - xi * hi, xr * hi + xi * hr))
    for c, value in enumerate(positions(products, inv2[...], inv1[...], turn_r, turn_i)):
        conv_ref[:, c] = value.astype(BF16).reshape(parts, units, width)

    channels = table_ref.shape[0]
    for h in range(128):
        folded[channels * h : channels * (h + 1), :] = table_ref[:, 256 * h : 256 * (h + 1)]
    high, low = lists(ask_ref)
    asked = high.shape[1]
    span, group = 256, 32
    for chunk in range(asked // span):
        cut = slice(span * chunk, span * (chunk + 1))
        onehot = lax.broadcasted_iota(I32, (256, span), 0) == low[:, cut]
        picked[...] = jnp.where(onehot, 1.0, 0.0).astype(BF16)
        row = jnp.broadcast_to(high[:, cut], (channels, span))

        def step(g, total):
            start = pl.multiple_of(g * group * channels, group * channels)
            all_high = dot(folded[pl.ds(start, group * channels), :], picked[...])
            for h in range(group):
                part = all_high[channels * h : channels * (h + 1)]
                total = total + jnp.where(row == g * group + h, part, 0.0)
            return total

        total = lax.fori_loop(0, 128 // group, step, jnp.zeros((channels, span), F32))
        for piece in range(span // 128):
            found_ref[chunk * (span // 128) + piece] = total[
                :, 128 * piece : 128 * (piece + 1)
            ].astype(BF16)


def onehot_places(place_ref, b, total):
    return jnp.where(
        lax.broadcasted_iota(I32, (total, 128), 0) == place_ref[b : b + 1, :], 1.0, 0.0
    ).astype(BF16)


def encode_body(
    scale, conv_ref, got_ref, place_ref, signal_ref, gate_ref, gain_ref, positive_ref,
    part_ref, pre_ref, enc_ref, embed_ref, scratch,
):
    channels, length = signal_ref.shape
    units = length // 128
    scratch[...] = conv_ref[...].reshape(channels * units, 128).astype(F32)
    parts = got_ref.shape[0]
    groups = place_ref.shape[0]
    rows = jnp.concatenate([got_ref[o] for o in range(parts)], axis=1)
    gain = gain_ref[...]
    for b in range(groups):
        embed = dot(rows, onehot_places(place_ref, b, parts * 128)).astype(BF16)
        embed_ref[:, 128 * b : 128 * (b + 1)] = embed
        tops = []
        for half in range(2):
            u = 2 * b + half
            cut = slice(128 * u, 128 * (u + 1))
            conv = scratch[pl.ds(u, channels, stride=units), :]
            pre = scale * conv + gain * signal_ref[:, cut].astype(F32)
            pre_ref[:, cut] = pre
            enc = (gate_ref[:, cut].astype(F32) * pre).astype(BF16)
            enc_ref[:, cut] = enc
            score = dot(embed, enc, TN)
            part_ref[b, 64 * half : 64 * (half + 1), :] = score[
                64 * half : 64 * (half + 1)
            ].astype(BF16)
            tops.append(
                jnp.sum(enc.astype(F32) * positive_ref[:, cut].astype(F32), axis=0, keepdims=True)
            )
        tops.append(jnp.zeros((14, 128), F32))
        part_ref[b, 128:, :] = jnp.concatenate(tops, axis=0).astype(BF16)


def weigh_body(scale, got_ref, out_ref):
    total = got_ref[0].astype(F32)
    for i in range(1, got_ref.shape[0]):
        total = total + got_ref[i].astype(F32)
    total = scale * total
    negative = total[:128]
    out_ref[:128, :] = (1.0 / (1.0 + jnp.exp(-negative))).astype(BF16)
    out_ref[128:, :] = (-1.0 / (1.0 + jnp.exp(total[128:]))).astype(BF16)


def back_body(
    scale, counts_ref, weight_ref, place_ref, embed_ref, enc_ref, pre_ref, gate_ref, positive_ref,
    send_ref, out_ref, grad_gate_ref, back_ref, scratch,
):
    channels, length = gate_ref.shape
    units = length // 128
    groups = place_ref.shape[0]
    parts = send_ref.shape[0]
    lane = lax.broadcasted_iota(I32, (channels, 128), 1)
    row = lax.broadcasted_iota(I32, (128, 128), 0)
    outgoing = jnp.zeros((channels, parts * 128), F32)
    for b in range(groups):
        limit = jnp.where(row < 64, counts_ref[2 * b], 64 + counts_ref[2 * b + 1])
        weight = jnp.where(row < limit, weight_ref[b, :128, :].astype(F32), 0.0).astype(BF16)
        top = weight_ref[b, 128:, :].astype(F32)
        embed = embed_ref[:, 128 * b : 128 * (b + 1)].astype(F32)
        slot = []
        for half in range(2):
            u = 2 * b + half
            cut = slice(128 * u, 128 * (u + 1))
            keep = (lane >= 64) if half else (lane < 64)
            masked = jnp.where(keep, embed, 0.0).astype(BF16)
            positive = positive_ref[:, cut].astype(F32)
            grad = scale * (top[half : half + 1, :] * positive + dot(masked, weight))
            grad_gate_ref[:, cut] = (grad * pre_ref[:, cut]).astype(BF16)
            back = grad * gate_ref[:, cut].astype(F32)
            back_ref[:, cut] = back
            scratch[pl.ds(u, channels, stride=units), :] = back
            slot.append(dot(enc_ref[:, cut], weight, NT))
        slot = (scale * jnp.where(lane < 64, slot[0], slot[1])).astype(BF16)
        outgoing = outgoing + dot(slot, onehot_places(place_ref, b, parts * 128), NT)
    for o in range(parts):
        out_ref[o] = outgoing[:, 128 * o : 128 * (o + 1)].astype(BF16)
    send_ref[...] = scratch[...].astype(BF16).reshape(send_ref.shape)


def lag_body(
    data_ref, spec_ref, fwd1, fwd2, inv2, inv1, turns, result_ref,
):
    parts, own, units, width = data_ref.shape
    turn_r, turn_i = turns[:, :N2], turns[:, N2:]
    columns = [data_ref[:, c].reshape(N1, N2) for c in range(own)]
    spectra = spectrum(columns, fwd1[...], fwd2[...], turn_r, turn_i)
    products = []
    for kind in (1, 0):
        for c in range(own):
            (br, bi), item = spectra[c], kind * own + c
            sr, si = spec_ref[item, 0], spec_ref[item, 1]
            products.append((sr * br + si * bi, sr * bi - si * br))
    for i, value in enumerate(positions(products, inv2[...], inv1[...], turn_r, turn_i)):
        result_ref[:, i // own, i % own] = value.astype(BF16).reshape(parts, units, width)


def table_body(in_ref, ask_ref, out_ref, columns):
    parts, channels, width = in_ref.shape
    high, low = lists(ask_ref)
    for s in range(parts):
        lows = jnp.broadcast_to(low[:, 128 * s : 128 * (s + 1)], (128, 128)).astype(F32).T
        lows = jnp.concatenate([lows, lows], axis=1)
        onehot = lows == lax.broadcasted_iota(I32, (128, 256), 1).astype(F32)
        columns[128 * s : 128 * (s + 1), :] = jnp.where(onehot, 1.0, 0.0).astype(BF16)
    values = jnp.concatenate([in_ref[s] for s in range(parts)], axis=1)
    row = jnp.broadcast_to(high.astype(F32).astype(BF16), values.shape)
    zero = jnp.zeros_like(values)
    group = 8

    @pl.loop(0, 128 // group)
    def _(g):
        base = (g * group).astype(F32)
        rows = [
            jnp.where(row == (base + h).astype(BF16), values, zero) for h in range(group)
        ]
        sums = dot(jnp.concatenate(rows, axis=0), columns[...])
        for h in range(group):
            start = pl.multiple_of((g * group + h) * 256, 256)
            out_ref[:, pl.ds(start, 256)] = sums[channels * h : channels * (h + 1)]


def last_body(scale, got_ref, back_ref, gain_ref, signal_ref, filter_ref, scratch):
    channels, length = back_ref.shape
    units = length // 128
    own = got_ref.shape[2]
    gain = gain_ref[...]
    for kind in range(2):
        scratch[kind] = got_ref[:, kind].reshape(channels * units, 128).astype(F32)
    for u in range(units):
        cut = slice(128 * u, 128 * (u + 1))
        rows = pl.ds(u, channels, stride=units)
        signal_ref[:, cut] = scale * scratch[0, rows, :] + gain * back_ref[:, cut]
        filter_ref[:, cut] = scale * scratch[1, rows, :]


def local(
    seq, chan, signal, gate_values, filter_taps, skip_gain, positive, item_table, item_row,
    negative_ids, block_counts,
):
    channels, length = signal.shape
    units, own = length // 128, channels // seq
    filter_scale, score_scale = (seq * length) ** -0.5, C**-0.5
    tables = [jnp.asarray(t) for t in transform_tables()]
    gain = jnp.broadcast_to(skip_gain[:, None], (channels, 128))
    rows = item_row[negative_ids].reshape(-1, 128)
    groups = rows.shape[0]
    flat = pltpu.VMEM((channels * units, 128), F32)

    data, ask, place = call(
        prep_body,
        [((seq, 2, own, units, 128), BF16), ((seq, 8, 128), F32), ((groups, 128), I32)],
        [flat],
        name="prep",
    )(rows, signal, filter_taps)
    data, ask = exchange([data, ask], "seq", seq, 1)
    conv, found, spec = call(
        forward_body,
        [
            ((seq, own, units, 128), BF16),
            ((seq, channels, 128), BF16),
            ((2 * own, 2, N1, N2), F32),
        ],
        [pltpu.VMEM((128 * channels, 256), BF16), pltpu.VMEM((256, 256), BF16)],
        name="forward",
    )(data, ask, item_table, *tables)
    conv, got = exchange([conv, found], "seq", seq, 2)
    part, pre, enc, embed = call(
        functools.partial(encode_body, filter_scale),
        [
            ((chan, 144, 128), BF16),
            ((channels, length), F32),
            ((channels, length), BF16),
            ((channels, groups * 128), BF16),
        ],
        [flat],
        name="encode",
    )(conv, got, place, signal, gate_values, gain, positive)
    (part,) = exchange([part], "chan", chan, 3)
    (weight,) = call(
        functools.partial(weigh_body, score_scale), [((144, 128), BF16)], name="weigh"
    )(part)
    (weight,) = exchange(
        [jnp.broadcast_to(weight[None], (chan, 144, 128))], "chan", chan, 4
    )
    send, out, grad_gate, back = call(
        functools.partial(back_body, score_scale),
        [
            ((seq, own, units, 128), BF16),
            ((seq, channels, 128), BF16),
            ((channels, length), BF16),
            ((channels, length), F32),
        ],
        [flat],
        specs=[SMEM] + [VMEM] * 7,
        name="back",
    )(block_counts, weight, place, embed, enc, pre, gate_values, positive)
    data, incoming = exchange([send, out], "seq", seq, 5)
    (result,) = call(lag_body, [((seq, 2, own, units, 128), BF16)], name="lag")(
        data, spec, *tables
    )
    (result,) = exchange([result], "seq", seq, 6)
    (grad_table,) = call(
        table_body,
        [((channels, item_table.shape[1]), F32)],
        [pltpu.VMEM((seq * 128, 256), BF16)],
        name="table",
    )(incoming, ask)
    grad_signal, grad_filter = call(
        functools.partial(last_body, filter_scale),
        [((channels, length), F32), ((channels, length), F32)],
        [pltpu.VMEM((2, channels * units, 128), F32)],
        name="last",
    )(result, back, gain)
    return grad_signal, grad_gate, grad_filter, grad_table


def solution(mesh):
    in_specs = (
        P("chan", "seq"),
        P("chan", "seq"),
        P("chan", "seq"),
        P("chan"),
        P("chan", "seq"),
        P("chan", "seq"),
        P(),
        P("seq", None),
        P("seq"),
    )
    out_specs = (P("chan", "seq"),) * 4
    body = functools.partial(local, mesh.shape["seq"], mesh.shape["chan"])
    return jax.shard_map(body, mesh=mesh, in_specs=in_specs, out_specs=out_specs, check_vma=False)
```

```python
import functools

import jax
import jax.numpy as jnp
import ml_dtypes
import numpy as np
from jax import lax
from jax.experimental import pallas as pl
from jax.experimental.pallas import tpu as pltpu
from jax.sharding import PartitionSpec as P

C = 256
F32, BF16, I32 = jnp.float32, jnp.bfloat16, jnp.int32
VMEM = pl.BlockSpec(memory_space=pltpu.VMEM)
SMEM = pl.BlockSpec(memory_space=pltpu.SMEM)
N1, N2 = 256, 128
LIMIT = 56 * 1024 * 1024
NT = (((1,), (1,)), ((), ()))
TN = (((0,), (0,)), ((), ()))


def halves(matrix):
    high = matrix.astype(ml_dtypes.bfloat16)
    return high, (matrix - high.astype(np.float64)).astype(ml_dtypes.bfloat16)


def transform_tables():
    total = N1 * N2
    k1, n1 = np.arange(N1) + 0.25, np.arange(N1)
    n2 = np.arange(N2)
    first = np.exp(-2j * np.pi * np.outer(k1, n1) / N1)
    turn = np.exp(-2j * np.pi * np.outer(k1, n2) / total)
    last = np.exp(-2j * np.pi * np.outer(n2, n2) / N2)
    fwd1 = np.concatenate(halves(np.concatenate([first.real, first.imag])), axis=1)
    fwd2 = np.block([[last.real, last.imag], [-last.imag, last.real]])
    inv2 = np.block([[last.real, -last.imag], [last.imag, last.real]])
    inv1 = np.concatenate([first.real.T, first.imag.T], axis=1) / total

    def stack_k(matrix):
        high, low = halves(matrix)
        return np.concatenate([high, high, low])

    high, low = halves(inv1)
    inv1 = np.concatenate([high, high, low], axis=1)
    turns = np.concatenate([turn.real, turn.imag], axis=1).astype(np.float32)
    return fwd1, stack_k(fwd2), stack_k(inv2), inv1, turns


def dot(left, right, dims=None):
    if dims is None:
        return jnp.dot(left, right, preferred_element_type=F32)
    return lax.dot_general(left, right, dims, preferred_element_type=F32)


def split(value):
    high = value.astype(BF16)
    return high, (value - high.astype(F32)).astype(BF16)


def spectrum(columns, fwd1, fwd2, turn_r, turn_i):
    joined = jnp.concatenate(columns, axis=1)
    stage = dot(fwd1, jnp.concatenate([joined, joined], axis=0))
    rows = []
    for item in range(len(columns)):
        real = stage[:N1, N2 * item : N2 * (item + 1)]
        imag = stage[N1:, N2 * item : N2 * (item + 1)]
        turned = jnp.concatenate(
            [real * turn_r - imag * turn_i, real * turn_i + imag * turn_r], axis=1
        )
        high, low = split(turned)
        rows.append(jnp.concatenate([high, low, high], axis=1))
    done = dot(jnp.concatenate(rows, axis=0), fwd2)
    return [
        (done[N1 * i : N1 * (i + 1), :N2], done[N1 * i : N1 * (i + 1), N2:])
        for i in range(len(columns))
    ]


def positions(spectra, inv2, inv1, turn_r, turn_i):
    rows = []
    for real, imag in spectra:
        high, low = split(jnp.concatenate([real, imag], axis=1))
        rows.append(jnp.concatenate([high, low, high], axis=1))
    stage = dot(jnp.concatenate(rows, axis=0), inv2)
    columns = []
    for item in range(len(spectra)):
        real = stage[N1 * item : N1 * (item + 1), :N2]
        imag = stage[N1 * item : N1 * (item + 1), N2:]
        columns.append(
            jnp.concatenate(
                [real * turn_r + imag * turn_i, imag * turn_r - real * turn_i], axis=0
            )
        )
    high, low = split(jnp.concatenate(columns, axis=1))
    done = dot(inv1, jnp.concatenate([high, low, high], axis=0))
    return [done[:, N2 * i : N2 * (i + 1)] for i in range(len(spectra))]


class Exchange:
    def __init__(self, axis, size, source, target, sems, one_piece=False):
        self.axis, self.size, self.source, self.target = axis, size, source, target
        self.send_sem, self.recv_sem = sems
        self.one_piece = one_piece

    def copy(self, step):
        me = lax.axis_index(self.axis)
        peer = lax.rem(me + step, self.size)
        return pltpu.make_async_remote_copy(
            src_ref=self.source if self.one_piece else self.source.at[peer],
            dst_ref=self.target.at[me],
            send_sem=self.send_sem.at[step],
            recv_sem=self.recv_sem.at[step],
            device_id={self.axis: peer},
            device_id_type=pl.DeviceIdType.MESH,
        )

    def start(self):
        @pl.loop(1, self.size)
        def _(step):
            self.copy(step).start()

        me = lax.axis_index(self.axis)
        self.target[me] = self.source[...] if self.one_piece else self.source[me]

    def wait(self):
        @pl.loop(1, self.size)
        def _(step):
            self.copy(step).wait()


def to_rows(value, scratch):
    channels, length = value.shape
    units = length // 128
    for u in range(units):
        scratch[pl.ds(u, channels, stride=units), :] = value[:, 128 * u : 128 * (u + 1)]
    return scratch[...]


def requests(rows, ask_ref, place_ref):
    parts = ask_ref.shape[0]
    groups = rows.shape[0]
    owner = rows >> 15
    high = ((rows >> 8) & 127).astype(F32)
    low = (rows & 255).astype(F32) + 1.0
    each = lax.broadcasted_iota(I32, (parts, 128), 0)
    onehots = [(owner[b : b + 1, :] == each).astype(F32) for b in range(groups)]
    stacked = jnp.concatenate(onehots, axis=0).astype(BF16)
    size = groups * parts
    above = lax.broadcasted_iota(I32, (128, 128), 0) < lax.broadcasted_iota(I32, (128, 128), 1)
    within = dot(stacked, above.astype(BF16))
    totals = dot(stacked, jnp.ones((128, 128), BF16))
    to, of = lax.broadcasted_iota(I32, (size, size), 0), lax.broadcasted_iota(I32, (size, size), 1)
    earlier = ((to - of) > 0) & (lax.rem(to + size - of, parts) == 0)
    rank = within + dot(earlier.astype(BF16), totals.astype(BF16))
    target = lax.broadcasted_iota(I32, (128, 128), 0).astype(F32)
    asked = jnp.zeros((2 * parts, 128), F32)
    for b in range(groups):
        mine = jnp.sum(onehots[b] * rank[parts * b : parts * (b + 1)], axis=0, keepdims=True)
        place_ref[b : b + 1, :] = owner[b : b + 1, :] * 128 + mine.astype(I32)
        ranks = (target == mine).astype(BF16)
        values = jnp.concatenate(
            [onehots[b] * high[b : b + 1, :], onehots[b] * low[b : b + 1, :]], axis=0
        )
        asked = asked + dot(values.astype(BF16), ranks, NT)
    asked = 256.0 * asked[:parts] + asked[parts:]
    for o in range(parts):
        ask_ref[o] = jnp.broadcast_to(asked[o : o + 1, :], (8, 128))


def lists(ask_ref):
    parts = ask_ref.shape[0]
    row = jnp.concatenate([ask_ref[s][0:1, :] for s in range(parts)], axis=1)
    row = row.astype(I32) - 1
    return row >> 8, row & 255


def find_rows(ask_ref, table_ref, folded, picked, found_ref):
    channels = table_ref.shape[0]
    for h in range(128):
        folded[channels * h : channels * (h + 1), :] = table_ref[:, 256 * h : 256 * (h + 1)]
    high, low = lists(ask_ref)
    asked = high.shape[1]
    span, group = 256, 32
    for chunk in range(asked // span):
        cut = slice(span * chunk, span * (chunk + 1))
        onehot = lax.broadcasted_iota(I32, (256, span), 0) == low[:, cut]
        picked[...] = jnp.where(onehot, 1.0, 0.0).astype(BF16)
        row = jnp.broadcast_to(high[:, cut], (channels, span))

        def step(g, total):
            start = pl.multiple_of(g * group * channels, group * channels)
            all_high = dot(folded[pl.ds(start, group * channels), :], picked[...])
            for h in range(group):
                part = all_high[channels * h : channels * (h + 1)]
                total = total + jnp.where(row == g * group + h, part, 0.0)
            return total

        total = lax.fori_loop(0, 128 // group, step, jnp.zeros((channels, span), F32))
        for piece in range(span // 128):
            found_ref[chunk * (span // 128) + piece] = total[
                :, 128 * piece : 128 * (piece + 1)
            ].astype(BF16)


def onehot_places(place_ref, b, total):
    return jnp.where(
        lax.broadcasted_iota(I32, (total, 128), 0) == place_ref[b : b + 1, :], 1.0, 0.0
    ).astype(BF16)


def add_rows(in_ref, ask_ref, columns, sums_ref, out_ref, sems):
    parts, channels, width = in_ref.shape
    high, low = lists(ask_ref)
    for s in range(parts):
        lows = jnp.broadcast_to(low[:, 128 * s : 128 * (s + 1)], (128, 128)).astype(F32).T
        lows = jnp.concatenate([lows, lows], axis=1)
        onehot = lows == lax.broadcasted_iota(I32, (128, 256), 1).astype(F32)
        columns[128 * s : 128 * (s + 1), :] = jnp.where(onehot, 1.0, 0.0).astype(BF16)
    values = jnp.concatenate([in_ref[s] for s in range(parts)], axis=1)
    row = jnp.broadcast_to(high.astype(F32).astype(BF16), values.shape)
    zero = jnp.zeros_like(values)
    group = sums_ref.shape[2] // 256

    def copy(g):
        start = pl.multiple_of(g * group * 256, group * 256)
        return pltpu.make_async_copy(
            sums_ref.at[g], out_ref.at[:, pl.ds(start, group * 256)], sems.at[g]
        )

    @pl.loop(0, 128 // group)
    def _(g):
        base = (g * group).astype(F32)
        rows = [
            jnp.where(row == (base + h).astype(BF16), values, zero) for h in range(group)
        ]
        sums = dot(jnp.concatenate(rows, axis=0), columns[...])
        for h in range(group):
            sums_ref[g, :, 256 * h : 256 * (h + 1)] = sums[channels * h : channels * (h + 1)]
        copy(g).start()

    return copy


def step_body(
    seq, chan, filter_scale, score_scale,
    ids_ref, counts_ref, lanes_ref, signal_ref, gate_ref, taps_ref, gain_ref, positive_ref,
    fwd1, fwd2, inv2, inv1, turns, table_hbm, item_hbm,
    grad_signal_ref, grad_gate_ref, grad_filter_ref, grad_table_hbm,
    data_s, data_r, ask_s, ask_r, conv_s, conv_r, found_s, found_r, part_s, part_r, weight_s, weight_r,
    gback_s, gback_r, out_s, out_r, res_s, res_r,
    place, flat, pre, enc, embed, back, spec, picked_rows, item, table, folded, picked, columns, sums,
    send_sems, recv_sems, local_sems, out_sems,
):
    channels, length = signal_ref.shape
    units = length // 128
    own = channels // seq
    groups = place.shape[0]

    def sems(i):
        return send_sems.at[i], recv_sems.at[i]

    data_x = Exchange("seq", seq, data_s, data_r, sems(0))
    ask_x = Exchange("seq", seq, ask_s, ask_r, sems(1))
    conv_x = Exchange("seq", seq, conv_s, conv_r, sems(2))
    found_x = Exchange("seq", seq, found_s, found_r, sems(3))
    part_x = Exchange("chan", chan, part_s, part_r, sems(4))
    weight_x = Exchange("chan", chan, weight_s, weight_r, sems(5), one_piece=True)
    gback_x = Exchange("seq", seq, gback_s, gback_r, sems(6))
    out_x = Exchange("seq", seq, out_s, out_r, sems(7))
    res_x = Exchange("seq", seq, res_s, res_r, sems(8))

    barrier = pltpu.get_barrier_semaphore()
    for axis, size in (("seq", seq), ("chan", chan)):
        me = lax.axis_index(axis)
        for step in range(1, size):
            pl.semaphore_signal(
                barrier,
                inc=1,
                device_id={axis: lax.rem(me + step, size)},
                device_id_type=pl.DeviceIdType.MESH,
            )
    item_copy = pltpu.make_async_copy(item_hbm, item, local_sems.at[0])
    table_copy = pltpu.make_async_copy(table_hbm, table, local_sems.at[1])
    item_copy.start()
    table_copy.start()

    for kind, ref in enumerate((signal_ref, taps_ref)):
        value = to_rows(ref[...].astype(F32), flat).astype(BF16)
        data_s[:, kind] = value.reshape(seq, own, units, 128)
    pl.semaphore_wait(barrier, seq + chan - 2)
    data_x.start()

    item_copy.wait()
    per = ids_ref.shape[1]

    @pl.loop(0, ids_ref.shape[0])
    def _(u):
        for j in range(per):
            picked_rows[pl.ds(u * per + j, 1), :] = item[pl.ds(ids_ref[u, j] >> 7, 1), :]

    lane_at = lanes_ref[...] & 127
    rows = []
    for b in range(groups):
        block = picked_rows[128 * b : 128 * (b + 1), :].astype(F32).T
        here = lax.broadcasted_iota(I32, (128, 128), 0) == lane_at[b : b + 1, :]
        rows.append(jnp.sum(jnp.where(here, block, 0.0), axis=0, keepdims=True))
    requests(jnp.concatenate(rows, axis=0).astype(I32), ask_s, place)
    ask_x.start()

    turn_r, turn_i = turns[:, :N2], turns[:, N2:]
    data_x.wait()
    spectra = spectrum(
        [data_r[:, kind, c].reshape(N1, N2) for kind in range(2) for c in range(own)],
        fwd1[...], fwd2[...], turn_r, turn_i,
    )
    for i, (real, imag) in enumerate(spectra):
        spec[i, 0] = real
        spec[i, 1] = imag
    products = []
    for c in range(own):
        (xr, xi), (hr, hi) = spectra[c], spectra[own + c]
        products.append((xr * hr - xi * hi, xr * hi + xi * hr))
    for c, value in enumerate(positions(products, inv2[...], inv1[...], turn_r, turn_i)):
        conv_s[:, c] = value.astype(BF16).reshape(seq, units, 128)
    conv_x.start()

    ask_x.wait()
    table_copy.wait()
    find_rows(ask_r, table, folded, picked, found_s)
    found_x.start()

    conv_x.wait()
    flat[...] = conv_r[...].reshape(channels * units, 128).astype(F32)
    square = lax.broadcasted_iota(I32, (channels, channels), 0) == lax.broadcasted_iota(
        I32, (channels, channels), 1
    )
    gain = jnp.sum(jnp.where(square, gain_ref[...], 0.0), axis=1, keepdims=True)
    tops = []
    for u in range(units):
        cut = slice(128 * u, 128 * (u + 1))
        conv = flat[pl.ds(u, channels, stride=units), :]
        value = filter_scale * conv + gain * signal_ref[:, cut].astype(F32)
        pre[:, cut] = value
        coded = (gate_ref[:, cut].astype(F32) * value).astype(BF16)
        enc[:, cut] = coded
        tops.append(
            jnp.sum(coded.astype(F32) * positive_ref[:, cut].astype(F32), axis=0, keepdims=True)
        )
    for b in range(groups):
        top = jnp.concatenate(tops[2 * b : 2 * b + 2] + [jnp.zeros((14, 128), F32)], axis=0)
        part_s[b, 128:, :] = top.astype(BF16)

    found_x.wait()
    found = jnp.concatenate([found_r[o] for o in range(seq)], axis=1)
    for b in range(groups):
        got = dot(found, onehot_places(place, b, seq * 128)).astype(BF16)
        embed[:, 128 * b : 128 * (b + 1)] = got
        for half in range(2):
            u = 2 * b + half
            score = dot(got, enc[:, 128 * u : 128 * (u + 1)], TN)
            rows = slice(64 * half, 64 * (half + 1))
            part_s[b, rows, :] = score[rows].astype(BF16)
    part_x.start()

    part_x.wait()
    total = part_r[0].astype(F32)
    for i in range(1, chan):
        total = total + part_r[i].astype(F32)
    total = score_scale * total
    weight_s[:128, :] = (1.0 / (1.0 + jnp.exp(-total[:128]))).astype(BF16)
    weight_s[128:, :] = (-1.0 / (1.0 + jnp.exp(total[128:]))).astype(BF16)
    weight_x.start()

    weight_x.wait()
    lane = lax.broadcasted_iota(I32, (channels, 128), 1)
    line = lax.broadcasted_iota(I32, (128, 128), 0)
    weights = []
    for b in range(groups):
        limit = jnp.where(line < 64, counts_ref[2 * b], 64 + counts_ref[2 * b + 1])
        weight = jnp.where(line < limit, weight_r[b, :128, :].astype(F32), 0.0).astype(BF16)
        weights.append(weight)
        top = weight_r[b, 128:, :].astype(F32)
        wide = embed[:, 128 * b : 128 * (b + 1)].astype(F32)
        for half in range(2):
            u = 2 * b + half
            cut = slice(128 * u, 128 * (u + 1))
            masked = jnp.where((lane >= 64) if half else (lane < 64), wide, 0.0).astype(BF16)
            positive = positive_ref[:, cut].astype(F32)
            grad = score_scale * (top[half : half + 1, :] * positive + dot(masked, weight))
            grad_gate_ref[:, cut] = (grad * pre[:, cut]).astype(BF16)
            value = grad * gate_ref[:, cut].astype(F32)
            back[:, cut] = gain * value
            flat[pl.ds(u, channels, stride=units), :] = value
    gback_s[...] = flat[...].astype(BF16).reshape(gback_s.shape)
    gback_x.start()

    outgoing = jnp.zeros((channels, seq * 128), F32)
    for b in range(groups):
        slot = [
            dot(enc[:, 128 * u : 128 * (u + 1)], weights[b], NT) for u in (2 * b, 2 * b + 1)
        ]
        slot = (score_scale * jnp.where(lane < 64, slot[0], slot[1])).astype(BF16)
        outgoing = outgoing + dot(slot, onehot_places(place, b, seq * 128), NT)
    for o in range(seq):
        out_s[o] = outgoing[:, 128 * o : 128 * (o + 1)].astype(BF16)
    out_x.start()

    gback_x.wait()
    spectra = spectrum(
        [gback_r[:, c].reshape(N1, N2) for c in range(own)], fwd1[...], fwd2[...], turn_r, turn_i
    )
    products = []
    for kind in (1, 0):
        for c in range(own):
            (br, bi), at = spectra[c], kind * own + c
            sr, si = spec[at, 0], spec[at, 1]
            products.append((sr * br + si * bi, sr * bi - si * br))
    for i, value in enumerate(positions(products, inv2[...], inv1[...], turn_r, turn_i)):
        res_s[:, i // own, i % own] = value.astype(BF16).reshape(seq, units, 128)
    res_x.start()

    out_x.wait()
    copy = add_rows(out_r, ask_r, columns, sums, grad_table_hbm, out_sems)
    res_x.wait()
    for kind, ref in enumerate((grad_signal_ref, grad_filter_ref)):
        flat[...] = res_r[:, kind].reshape(channels * units, 128).astype(F32)
        for u in range(units):
            cut = slice(128 * u, 128 * (u + 1))
            value = filter_scale * flat[pl.ds(u, channels, stride=units), :]
            ref[:, cut] = value + back[:, cut] if kind == 0 else value

    @pl.loop(0, sums.shape[0])
    def _(g):
        copy(g).wait()


def local(
    seq, chan, signal, gate_values, filter_taps, skip_gain, positive, item_table, item_row,
    negative_ids, block_counts,
):
    channels, length = signal.shape
    units, own = length // 128, channels // seq
    rows_own = item_table.shape[1]
    slots = negative_ids.size
    groups = slots // 128
    table_groups = 4
    tables = [jnp.asarray(t) for t in transform_tables()]
    seq_pair = lambda *shape: [pltpu.VMEM((seq, *shape), BF16)] * 2
    scratch = [
        *seq_pair(2, own, units, 128),
        *[pltpu.VMEM((seq, 8, 128), F32)] * 2,
        *seq_pair(own, units, 128),
        *seq_pair(channels, 128),
        *[pltpu.VMEM((chan, 144, 128), BF16)] * 2,
        pltpu.VMEM((144, 128), BF16),
        pltpu.VMEM((chan, 144, 128), BF16),
        *seq_pair(own, units, 128),
        *seq_pair(channels, 128),
        *seq_pair(2, own, units, 128),
        pltpu.VMEM((groups, 128), I32),
        pltpu.VMEM((channels * units, 128), F32),
        pltpu.VMEM((channels, length), F32),
        pltpu.VMEM((channels, length), BF16),
        pltpu.VMEM((channels, slots), BF16),
        pltpu.VMEM((channels, length), F32),
        pltpu.VMEM((2 * own, 2, N1, N2), F32),
        pltpu.VMEM((slots, 128), I32),
        pltpu.VMEM((item_row.size // 128, 128), I32),
        pltpu.VMEM((channels, rows_own), BF16),
        pltpu.VMEM((channels * rows_own // 256, 256), BF16),
        pltpu.VMEM((256, 256), BF16),
        pltpu.VMEM((seq * 128, 256), BF16),
        pltpu.VMEM((table_groups, channels, rows_own // table_groups), F32),
        pltpu.SemaphoreType.DMA((9, seq)),
        pltpu.SemaphoreType.DMA((9, seq)),
        pltpu.SemaphoreType.DMA((2,)),
        pltpu.SemaphoreType.DMA((table_groups,)),
    ]
    any_space = pl.BlockSpec(memory_space=pl.ANY)
    return pl.pallas_call(
        functools.partial(step_body, seq, chan, (seq * length) ** -0.5, C**-0.5),
        out_shape=[
            jax.ShapeDtypeStruct((channels, length), F32),
            jax.ShapeDtypeStruct((channels, length), BF16),
            jax.ShapeDtypeStruct((channels, length), F32),
            jax.ShapeDtypeStruct((channels, rows_own), F32),
        ],
        in_specs=[SMEM] * 2 + [VMEM] * 11 + [any_space] * 2,
        out_specs=[VMEM] * 3 + [any_space],
        scratch_shapes=scratch,
        compiler_params=pltpu.CompilerParams(
            collective_id=1, has_side_effects=True, vmem_limit_bytes=LIMIT
        ),
        name="step",
    )(
        negative_ids, block_counts, negative_ids.reshape(groups, 128), signal, gate_values,
        filter_taps, skip_gain.reshape(1, channels), positive, *tables, item_table,
        item_row.reshape(-1, 128),
    )


def solution(mesh):
    in_specs = (
        P("chan", "seq"),
        P("chan", "seq"),
        P("chan", "seq"),
        P("chan"),
        P("chan", "seq"),
        P("chan", "seq"),
        P(),
        P("seq", None),
        P("seq"),
    )
    out_specs = (P("chan", "seq"),) * 4
    body = functools.partial(local, mesh.shape["seq"], mesh.shape["chan"])
    return jax.shard_map(body, mesh=mesh, in_specs=in_specs, out_specs=out_specs, check_vma=False)
```

```python
import functools

import jax
import jax.numpy as jnp
import ml_dtypes
import numpy as np
from jax import lax
from jax.experimental import pallas as pl
from jax.experimental.pallas import tpu as pltpu
from jax.sharding import PartitionSpec as P

C = 256
F32, BF16, I32 = jnp.float32, jnp.bfloat16, jnp.int32
VMEM = pl.BlockSpec(memory_space=pltpu.VMEM)
SMEM = pl.BlockSpec(memory_space=pltpu.SMEM)
ANY = pl.BlockSpec(memory_space=pl.ANY)
N1, N2 = 256, 128
LOW_BITS = 9
LOW = 1 << LOW_BITS
LIMIT = 56 * 1024 * 1024
NT = (((1,), (1,)), ((), ()))
TN = (((0,), (0,)), ((), ()))


def halves(matrix):
    high = matrix.astype(ml_dtypes.bfloat16)
    return high, (matrix - high.astype(np.float64)).astype(ml_dtypes.bfloat16)


def transform_tables():
    total = N1 * N2
    k1, n1 = np.arange(N1) + 0.25, np.arange(N1)
    n2 = np.arange(N2)
    first = np.exp(-2j * np.pi * np.outer(k1, n1) / N1)
    turn = np.exp(-2j * np.pi * np.outer(k1, n2) / total)
    last = np.exp(-2j * np.pi * np.outer(n2, n2) / N2)
    fwd1 = np.concatenate(halves(np.concatenate([first.real, first.imag])), axis=1)
    fwd2 = np.block([[last.real, last.imag], [-last.imag, last.real]])
    inv2 = np.block([[last.real, -last.imag], [last.imag, last.real]])
    inv1 = np.concatenate([first.real.T, first.imag.T], axis=1) / total

    def stack_k(matrix):
        high, low = halves(matrix)
        return np.concatenate([high, high, low])

    high, low = halves(inv1)
    inv1 = np.concatenate([high, high, low], axis=1)
    turns = np.concatenate([turn.real, turn.imag], axis=1).astype(np.float32)
    return fwd1, stack_k(fwd2), stack_k(inv2), inv1, turns


def dot(left, right, dims=None):
    if dims is None:
        return jnp.dot(left, right, preferred_element_type=F32)
    return lax.dot_general(left, right, dims, preferred_element_type=F32)


def split(value):
    high = value.astype(BF16)
    return high, (value - high.astype(F32)).astype(BF16)


def spectrum(columns, fwd1, fwd2, turn_r, turn_i):
    joined = jnp.concatenate(columns, axis=1)
    stage = dot(fwd1, jnp.concatenate([joined, joined], axis=0))
    rows = []
    for item in range(len(columns)):
        real = stage[:N1, N2 * item : N2 * (item + 1)]
        imag = stage[N1:, N2 * item : N2 * (item + 1)]
        turned = jnp.concatenate(
            [real * turn_r - imag * turn_i, real * turn_i + imag * turn_r], axis=1
        )
        high, low = split(turned)
        rows.append(jnp.concatenate([high, low, high], axis=1))
    done = dot(jnp.concatenate(rows, axis=0), fwd2)
    return [
        (done[N1 * i : N1 * (i + 1), :N2], done[N1 * i : N1 * (i + 1), N2:])
        for i in range(len(columns))
    ]


def positions(spectra, inv2, inv1, turn_r, turn_i):
    rows = []
    for real, imag in spectra:
        high, low = split(jnp.concatenate([real, imag], axis=1))
        rows.append(jnp.concatenate([high, low, high], axis=1))
    stage = dot(jnp.concatenate(rows, axis=0), inv2)
    columns = []
    for item in range(len(spectra)):
        real = stage[N1 * item : N1 * (item + 1), :N2]
        imag = stage[N1 * item : N1 * (item + 1), N2:]
        columns.append(
            jnp.concatenate(
                [real * turn_r + imag * turn_i, imag * turn_r - real * turn_i], axis=0
            )
        )
    high, low = split(jnp.concatenate(columns, axis=1))
    done = dot(inv1, jnp.concatenate([high, low, high], axis=0))
    return [done[:, N2 * i : N2 * (i + 1)] for i in range(len(spectra))]


class Exchange:
    def __init__(self, axis, size, source, target, sems, one_piece=False):
        self.axis, self.size, self.source, self.target = axis, size, source, target
        self.send_sem, self.recv_sem = sems
        self.one_piece = one_piece

    def copy(self, step):
        me = lax.axis_index(self.axis)
        peer = lax.rem(me + step, self.size)
        return pltpu.make_async_remote_copy(
            src_ref=self.source if self.one_piece else self.source.at[peer],
            dst_ref=self.target.at[me],
            send_sem=self.send_sem.at[step],
            recv_sem=self.recv_sem.at[step],
            device_id={self.axis: peer},
            device_id_type=pl.DeviceIdType.MESH,
        )

    def start(self):
        @pl.loop(1, self.size)
        def _(step):
            self.copy(step).start()

        me = lax.axis_index(self.axis)
        self.target[me] = self.source[...] if self.one_piece else self.source[me]

    def wait(self):
        @pl.loop(1, self.size)
        def _(step):
            self.copy(step).wait()


def to_rows(value, scratch):
    channels, length = value.shape
    units = length // 128
    for u in range(units):
        scratch[pl.ds(u, channels, stride=units), :] = value[:, 128 * u : 128 * (u + 1)]
    return scratch[...]


def requests(rows, turned, ask_ref, place_ref):
    parts = ask_ref.shape[0]
    groups = rows.shape[0]
    owner = rows >> 15
    high = ((rows >> 8) & 127).astype(F32)
    low = (rows & 255).astype(F32) + 1.0
    each = lax.broadcasted_iota(I32, (parts, 128), 0)
    onehots = [(owner[b : b + 1, :] == each).astype(F32) for b in range(groups)]
    stacked = jnp.concatenate(onehots, axis=0).astype(BF16)
    size = groups * parts
    above = lax.broadcasted_iota(I32, (128, 128), 0) < lax.broadcasted_iota(I32, (128, 128), 1)
    within = dot(stacked, above.astype(BF16))
    totals = dot(stacked, jnp.ones((128, 128), BF16))
    to, of = lax.broadcasted_iota(I32, (size, size), 0), lax.broadcasted_iota(I32, (size, size), 1)
    earlier = ((to - of) > 0) & (lax.rem(to + size - of, parts) == 0)
    rank = within + dot(earlier.astype(BF16), totals.astype(BF16))
    target = lax.broadcasted_iota(I32, (128, 128), 0).astype(F32)
    asked = jnp.zeros((2 * parts, 128), F32)
    for b in range(groups):
        mine = jnp.sum(onehots[b] * rank[parts * b : parts * (b + 1)], axis=0, keepdims=True)
        at = (mine.astype(I32) + turned) & 127
        place_ref[b : b + 1, :] = owner[b : b + 1, :] * 128 + at
        ranks = (target == at.astype(F32)).astype(BF16)
        values = jnp.concatenate(
            [onehots[b] * high[b : b + 1, :], onehots[b] * low[b : b + 1, :]], axis=0
        )
        asked = asked + dot(values.astype(BF16), ranks, NT)
    asked = 256.0 * asked[:parts] + asked[parts:]
    for o in range(parts):
        ask_ref[o] = jnp.broadcast_to(asked[o : o + 1, :], (8, 128))


def packed(pieces):
    lane = lax.broadcasted_iota(I32, pieces[0].shape, 1)
    out = []
    for first in range(0, len(pieces), 4):
        p = pieces[first : first + 4]
        out += [jnp.where(lane < cut, p[i], p[i + 1]) for i, cut in enumerate((96, 64, 32))]
    return jnp.concatenate(out, axis=1)


def unpacked(joined):
    t = [joined[:, 128 * i : 128 * (i + 1)] for i in range(3)]
    lane = lax.broadcasted_iota(I32, t[0].shape, 1)
    return [t[0], jnp.where(lane < 96, t[1], t[0]), jnp.where(lane < 64, t[2], t[1]), t[2]]


def lists(ask_ref):
    row = packed([ask_ref[s][0:1, :] for s in range(ask_ref.shape[0])])
    row = row.astype(I32) - 1
    return row >> LOW_BITS, row & (LOW - 1)


def find_rows(ask_ref, table_ref, folded, picked, row_found, found_ref):
    channels, rows_own = table_ref.shape
    highs = rows_own // LOW
    for h in range(highs):
        folded[channels * h : channels * (h + 1), :] = table_ref[:, LOW * h : LOW * (h + 1)]
    high, low = lists(ask_ref)
    asked = high.shape[1]
    span, group = 512, 32
    for chunk in range(asked // span):
        cut = slice(span * chunk, span * (chunk + 1))
        onehot = lax.broadcasted_iota(I32, (LOW, span), 0) == low[:, cut]
        picked[...] = jnp.where(onehot, 1.0, 0.0).astype(BF16)
        row = jnp.broadcast_to(high[:, cut], (channels, span))

        def step(g, total):
            start = pl.multiple_of(g * group * channels, group * channels)
            all_high = dot(folded[pl.ds(start, group * channels), :], picked[...])
            for h in range(group):
                part = all_high[channels * h : channels * (h + 1)]
                total = total + jnp.where(row == g * group + h, part, 0.0)
            return total

        row_found[:, cut] = lax.fori_loop(
            0, highs // group, step, jnp.zeros((channels, span), F32)
        )
    for first in range(0, found_ref.shape[0], 4):
        pieces = unpacked(row_found[:, 96 * first : 96 * (first + 4)])
        for i, piece in enumerate(pieces):
            found_ref[first + i] = piece.astype(BF16)


def onehot_places(place_ref, b, total):
    return jnp.where(
        lax.broadcasted_iota(I32, (total, 128), 0) == place_ref[b : b + 1, :], 1.0, 0.0
    ).astype(BF16)


def add_rows(in_ref, ask_ref, columns, sums_ref, out_ref, sems):
    parts, channels, width = in_ref.shape
    high, low = lists(ask_ref)
    for s in range(low.shape[1] // 128):
        lows = jnp.broadcast_to(low[:, 128 * s : 128 * (s + 1)], (128, 128)).astype(F32).T
        lows = jnp.concatenate([lows] * (LOW // 128), axis=1)
        onehot = lows == lax.broadcasted_iota(I32, (128, LOW), 1).astype(F32)
        columns[128 * s : 128 * (s + 1), :] = jnp.where(onehot, 1.0, 0.0).astype(BF16)
    values = packed([in_ref[s].astype(F32) for s in range(parts)]).astype(BF16)
    row = jnp.broadcast_to(high.astype(F32).astype(BF16), values.shape)
    zero = jnp.zeros_like(values)
    groups = sums_ref.shape[0]
    group = sums_ref.shape[2] // LOW

    def copy(g):
        return pltpu.make_async_copy(sums_ref.at[g], out_ref.at[g], sems.at[g])

    @pl.loop(0, groups)
    def _(g):
        base = (g * group).astype(F32)
        rows = [
            jnp.where(row == (base + h).astype(BF16), values, zero) for h in range(group)
        ]
        sums = dot(jnp.concatenate(rows, axis=0), columns[...])
        for h in range(group):
            sums_ref[g, :, LOW * h : LOW * (h + 1)] = sums[channels * h : channels * (h + 1)]
        copy(g).start()

    return copy


def step_body(
    seq, chan, filter_scale, score_scale,
    ids_ref, counts_ref, lanes_ref, signal_ref, taps_ref, gain_ref, *refs,
):
    later_hbm, refs = refs[:9], refs[9:]
    lag_ref, back, grad_gate_ref, grad_table_hbm = refs[:4]
    (
    data_s, data_r, ask_s, ask_r, conv_s, conv_r, found_s, found_r, part_s, part_r, weight_s, weight_r,
    gback_s, gback_r, out_s, out_r, res_s, res_r,
    place, flat, pre, enc, embed, spec, picked_rows, folded, picked, row_found, columns, sums,
    send_sems, recv_sems, local_sems, out_sems,
    *later,
    ) = refs[4:]
    item, fwd1, fwd2, inv2, inv1, turns, gate_ref, positive_ref, table = later
    channels, length = signal_ref.shape
    units = length // 128
    own = channels // seq
    groups = place.shape[0]

    def sems(i):
        return send_sems.at[i], recv_sems.at[i]

    data_x = Exchange("seq", seq, data_s, data_r, sems(0))
    ask_x = Exchange("seq", seq, ask_s, ask_r, sems(1))
    conv_x = Exchange("seq", seq, conv_s, conv_r, sems(2))
    found_x = Exchange("seq", seq, found_s, found_r, sems(3))
    part_x = Exchange("chan", chan, part_s, part_r, sems(4))
    weight_x = Exchange("chan", chan, weight_s, weight_r, sems(5), one_piece=True)
    gback_x = Exchange("seq", seq, gback_s, gback_r, sems(6))
    out_x = Exchange("seq", seq, out_s, out_r, sems(7))
    res_x = Exchange("seq", seq, res_s, res_r, sems(8))

    barrier = pltpu.get_barrier_semaphore()
    for axis, size in (("seq", seq), ("chan", chan)):
        me = lax.axis_index(axis)
        for step in range(1, size):
            pl.semaphore_signal(
                barrier,
                inc=1,
                device_id={axis: lax.rem(me + step, size)},
                device_id_type=pl.DeviceIdType.MESH,
            )
    loads = [
        pltpu.make_async_copy(s, t, local_sems.at[i])
        for i, (s, t) in enumerate(zip(later_hbm, later))
    ]
    for load in loads:
        load.start()

    for kind, ref in enumerate((signal_ref, taps_ref)):
        value = to_rows(ref[...].astype(F32), flat).astype(BF16)
        data_s[:, kind] = value.reshape(seq, own, units, 128)
    pl.semaphore_wait(barrier, seq + chan - 2)
    data_x.start()

    loads[0].wait()
    per = ids_ref.shape[1]

    @pl.loop(0, ids_ref.shape[0])
    def _(u):
        for j in range(per):
            picked_rows[pl.ds(u * per + j, 1), :] = item[pl.ds(ids_ref[u, j] >> 7, 1), :]

    rows = []
    ids = lanes_ref[...].astype(F32)
    lane_at = jnp.concatenate(
        [
            jnp.concatenate([ids[2 * b : 2 * b + 1], ids[2 * b + 1 : 2 * b + 2]], axis=1)
            for b in range(groups)
        ],
        axis=0,
    )
    lane_at = lane_at.astype(I32) & 127
    for b in range(groups):
        block = picked_rows[128 * b : 128 * (b + 1), :].astype(F32).T
        here = lax.broadcasted_iota(I32, (128, 128), 0) == lane_at[b : b + 1, :]
        rows.append(jnp.sum(jnp.where(here, block, 0.0), axis=0, keepdims=True))
    turned = (96 * lax.axis_index("seq")) & 127
    requests(jnp.concatenate(rows, axis=0).astype(I32), turned, ask_s, place)
    ask_x.start()

    for load in loads[1:6]:
        load.wait()
    turn_r, turn_i = turns[:, :N2], turns[:, N2:]
    data_x.wait()
    spectra = spectrum(
        [data_r[:, kind, c].reshape(N1, N2) for kind in range(2) for c in range(own)],
        fwd1[...], fwd2[...], turn_r, turn_i,
    )
    for i, (real, imag) in enumerate(spectra):
        spec[i, 0] = real
        spec[i, 1] = imag
    products = []
    for c in range(own):
        (xr, xi), (hr, hi) = spectra[c], spectra[own + c]
        products.append((xr * hr - xi * hi, xr * hi + xi * hr))
    for c, value in enumerate(positions(products, inv2[...], inv1[...], turn_r, turn_i)):
        conv_s[:, c] = value.astype(BF16).reshape(seq, units, 128)
    conv_x.start()

    ask_x.wait()
    for load in loads[6:]:
        load.wait()
    find_rows(ask_r, table, folded, picked, row_found, found_s)
    found_x.start()

    conv_x.wait()
    flat[...] = conv_r[...].reshape(channels * units, 128).astype(F32)
    square = lax.broadcasted_iota(I32, (channels, channels), 0) == lax.broadcasted_iota(
        I32, (channels, channels), 1
    )
    gain = jnp.sum(jnp.where(square, gain_ref[...], 0.0), axis=1, keepdims=True)
    tops = []
    for u in range(units):
        cut = slice(128 * u, 128 * (u + 1))
        conv = flat[pl.ds(u, channels, stride=units), :]
        value = filter_scale * conv + gain * signal_ref[:, cut].astype(F32)
        pre[:, cut] = value
        coded = (gate_ref[:, cut].astype(F32) * value).astype(BF16)
        enc[:, cut] = coded
        tops.append(
            jnp.sum(coded.astype(F32) * positive_ref[:, cut].astype(F32), axis=0, keepdims=True)
        )
    for b in range(groups):
        top = jnp.concatenate(tops[2 * b : 2 * b + 2] + [jnp.zeros((14, 128), F32)], axis=0)
        part_s[b, 128:, :] = top.astype(BF16)

    found_x.wait()
    found = jnp.concatenate([found_r[o] for o in range(seq)], axis=1)
    for b in range(groups):
        got = dot(found, onehot_places(place, b, seq * 128)).astype(BF16)
        embed[:, 128 * b : 128 * (b + 1)] = got
        for half in range(2):
            u = 2 * b + half
            score = dot(got, enc[:, 128 * u : 128 * (u + 1)], TN)
            rows = slice(64 * half, 64 * (half + 1))
            part_s[b, rows, :] = score[rows].astype(BF16)
    part_x.start()

    part_x.wait()
    total = part_r[0].astype(F32)
    for i in range(1, chan):
        total = total + part_r[i].astype(F32)
    total = score_scale * total
    weight_s[:128, :] = (1.0 / (1.0 + jnp.exp(-total[:128]))).astype(BF16)
    weight_s[128:, :] = (-1.0 / (1.0 + jnp.exp(total[128:]))).astype(BF16)
    weight_x.start()

    weight_x.wait()
    lane = lax.broadcasted_iota(I32, (channels, 128), 1)
    line = lax.broadcasted_iota(I32, (128, 128), 0)
    weights = []
    for b in range(groups):
        limit = jnp.where(line < 64, counts_ref[2 * b], 64 + counts_ref[2 * b + 1])
        weight = jnp.where(line < limit, weight_r[b, :128, :].astype(F32), 0.0).astype(BF16)
        weights.append(weight)
        top = weight_r[b, 128:, :].astype(F32)
        wide = embed[:, 128 * b : 128 * (b + 1)].astype(F32)
        for half in range(2):
            u = 2 * b + half
            cut = slice(128 * u, 128 * (u + 1))
            masked = jnp.where((lane >= 64) if half else (lane < 64), wide, 0.0).astype(BF16)
            positive = positive_ref[:, cut].astype(F32)
            grad = score_scale * (top[half : half + 1, :] * positive + dot(masked, weight))
            grad_gate_ref[:, cut] = (grad * pre[:, cut]).astype(BF16)
            value = grad * gate_ref[:, cut].astype(F32)
            back[:, cut] = gain * value
            flat[pl.ds(u, channels, stride=units), :] = value
    gback_s[...] = flat[...].astype(BF16).reshape(gback_s.shape)
    gback_x.start()

    outgoing = jnp.zeros((channels, seq * 128), F32)
    for b in range(groups):
        slot = [
            dot(enc[:, 128 * u : 128 * (u + 1)], weights[b], NT) for u in (2 * b, 2 * b + 1)
        ]
        slot = (score_scale * jnp.where(lane < 64, slot[0], slot[1])).astype(BF16)
        outgoing = outgoing + dot(slot, onehot_places(place, b, seq * 128), NT)
    for o in range(seq):
        out_s[o] = outgoing[:, 128 * o : 128 * (o + 1)].astype(BF16)
    out_x.start()

    gback_x.wait()
    spectra = spectrum(
        [gback_r[:, c].reshape(N1, N2) for c in range(own)], fwd1[...], fwd2[...], turn_r, turn_i
    )
    products = []
    for kind in (1, 0):
        for c in range(own):
            (br, bi), at = spectra[c], kind * own + c
            sr, si = spec[at, 0], spec[at, 1]
            products.append((sr * br + si * bi, sr * bi - si * br))
    for i, value in enumerate(positions(products, inv2[...], inv1[...], turn_r, turn_i)):
        res_s[:, i // own, i % own] = value.astype(BF16).reshape(seq, units, 128)
    res_x.start()

    out_x.wait()
    copy = add_rows(out_r, ask_r, columns, sums, grad_table_hbm, out_sems)
    res_x.wait()
    lag_ref[...] = res_r[...]

    @pl.loop(0, sums.shape[0])
    def _(g):
        copy(g).wait()


def last_body(
    scale, lag_ref, back_ref, gate_ref, table_hbm,
    grad_signal_ref, grad_gate_ref, grad_filter_ref, grad_table_hbm, flat, held, in_sems, out_sems,
):
    groups, _, width = table_hbm.shape
    pieces, _, span = held.shape
    loads, copies = [], []
    for i in range(pieces):
        g, start = divmod(span * i, width)
        loads.append(
            pltpu.make_async_copy(
                table_hbm.at[g, :, start : start + span], held.at[i], in_sems.at[i]
            )
        )
        copies.append(
            pltpu.make_async_copy(
                held.at[i], grad_table_hbm.at[:, span * i : span * (i + 1)], out_sems.at[i]
            )
        )
    for load in loads:
        load.start()
    grad_gate_ref[...] = gate_ref[...]
    channels, length = back_ref.shape
    units = length // 128
    for kind, ref in enumerate((grad_signal_ref, grad_filter_ref)):
        flat[...] = lag_ref[:, kind].reshape(channels * units, 128).astype(F32)
        for u in range(units):
            cut = slice(128 * u, 128 * (u + 1))
            value = scale * flat[pl.ds(u, channels, stride=units), :]
            ref[:, cut] = value + back_ref[:, cut] if kind == 0 else value
        for i in range(pieces // 2 * kind, pieces // 2 * (kind + 1)):
            loads[i].wait()
            copies[i].start()
    for copy in copies:
        copy.wait()


def local(
    seq, chan, signal, gate_values, filter_taps, skip_gain, positive, item_table, item_row,
    negative_ids, block_counts,
):
    channels, length = signal.shape
    units, own = length // 128, channels // seq
    rows_own = item_table.shape[1]
    slots = negative_ids.size
    groups = slots // 128
    table_groups = 2
    tables = [jnp.asarray(t) for t in transform_tables()]
    later = [item_row.reshape(-1, 128), *tables, gate_values, positive, item_table]
    seq_pair = lambda *shape: [pltpu.VMEM((seq, *shape), BF16)] * 2
    scratch = [
        *seq_pair(2, own, units, 128),
        *[pltpu.VMEM((seq, 8, 128), F32)] * 2,
        *seq_pair(own, units, 128),
        *seq_pair(channels, 128),
        *[pltpu.VMEM((chan, 144, 128), BF16)] * 2,
        pltpu.VMEM((144, 128), BF16),
        pltpu.VMEM((chan, 144, 128), BF16),
        *seq_pair(own, units, 128),
        *seq_pair(channels, 128),
        *seq_pair(2, own, units, 128),
        pltpu.VMEM((groups, 128), I32),
        pltpu.VMEM((channels * units, 128), F32),
        pltpu.VMEM((channels, length), F32),
        pltpu.VMEM((channels, length), BF16),
        pltpu.VMEM((channels, slots), BF16),
        pltpu.VMEM((2 * own, 2, N1, N2), F32),
        pltpu.VMEM((slots, 128), I32),
        pltpu.VMEM((channels * rows_own // LOW, LOW), BF16),
        pltpu.VMEM((LOW, 512), BF16),
        pltpu.VMEM((channels, seq * 96), F32),
        pltpu.VMEM((seq * 96, LOW), BF16),
        pltpu.VMEM((table_groups, channels, rows_own // table_groups), F32),
        pltpu.SemaphoreType.DMA((9, seq)),
        pltpu.SemaphoreType.DMA((9, seq)),
        pltpu.SemaphoreType.DMA((len(later),)),
        pltpu.SemaphoreType.DMA((table_groups,)),
        *[pltpu.VMEM(a.shape, a.dtype) for a in later],
    ]
    lag, back, gate, table = pl.pallas_call(
        functools.partial(step_body, seq, chan, (seq * length) ** -0.5, C**-0.5),
        out_shape=[
            jax.ShapeDtypeStruct((seq, 2, own, units, 128), BF16),
            jax.ShapeDtypeStruct((channels, length), F32),
            jax.ShapeDtypeStruct((channels, length), BF16),
            jax.ShapeDtypeStruct((table_groups, channels, rows_own // table_groups), F32),
        ],
        in_specs=[SMEM] * 2 + [VMEM] * 4 + [ANY] * len(later),
        out_specs=[VMEM] * 3 + [ANY],
        scratch_shapes=scratch,
        compiler_params=pltpu.CompilerParams(
            collective_id=1, has_side_effects=True, vmem_limit_bytes=LIMIT
        ),
        name="step",
    )(
        negative_ids, block_counts, negative_ids, signal, filter_taps,
        skip_gain.reshape(1, channels), *later,
    )
    return pl.pallas_call(
        functools.partial(last_body, (seq * length) ** -0.5),
        out_shape=[
            jax.ShapeDtypeStruct((channels, length), F32),
            jax.ShapeDtypeStruct((channels, length), BF16),
            jax.ShapeDtypeStruct((channels, length), F32),
            jax.ShapeDtypeStruct((channels, rows_own), F32),
        ],
        in_specs=[VMEM] * 3 + [ANY],
        out_specs=[VMEM] * 3 + [ANY],
        scratch_shapes=[
            pltpu.VMEM((channels * units, 128), F32),
            pltpu.VMEM((8, channels, rows_own // 8), F32),
            pltpu.SemaphoreType.DMA((8,)),
            pltpu.SemaphoreType.DMA((8,)),
        ],
        compiler_params=pltpu.CompilerParams(vmem_limit_bytes=LIMIT),
        name="last",
    )(lag, back, gate, table)


def solution(mesh):
    in_specs = (
        P("chan", "seq"),
        P("chan", "seq"),
        P("chan", "seq"),
        P("chan"),
        P("chan", "seq"),
        P("chan", "seq"),
        P(),
        P("seq", None),
        P("seq"),
    )
    out_specs = (P("chan", "seq"),) * 4
    body = functools.partial(local, mesh.shape["seq"], mesh.shape["chan"])
    return jax.shard_map(body, mesh=mesh, in_specs=in_specs, out_specs=out_specs, check_vma=False)
```

```python
import functools

import jax
import jax.numpy as jnp
import ml_dtypes
import numpy as np
from jax import lax
from jax.experimental import pallas as pl
from jax.experimental.pallas import tpu as pltpu
from jax.sharding import PartitionSpec as P

C = 256
F32, BF16, I32 = jnp.float32, jnp.bfloat16, jnp.int32
VMEM = pl.BlockSpec(memory_space=pltpu.VMEM)
SMEM = pl.BlockSpec(memory_space=pltpu.SMEM)
ANY = pl.BlockSpec(memory_space=pl.ANY)
N1, N2 = 256, 128
LOW_BITS = 9
LOW = 1 << LOW_BITS
LIMIT = 56 * 1024 * 1024
NT = (((1,), (1,)), ((), ()))
TN = (((0,), (0,)), ((), ()))


def halves(matrix):
    high = matrix.astype(ml_dtypes.bfloat16)
    return high, (matrix - high.astype(np.float64)).astype(ml_dtypes.bfloat16)


def transform_tables():
    total = N1 * N2
    k1, n1 = np.arange(N1) + 0.25, np.arange(N1)
    n2 = np.arange(N2)
    first = np.exp(-2j * np.pi * np.outer(k1, n1) / N1)
    turn = np.exp(-2j * np.pi * np.outer(k1, n2) / total)
    last = np.exp(-2j * np.pi * np.outer(n2, n2) / N2)
    fwd1 = np.concatenate(halves(np.concatenate([first.real, first.imag])), axis=1)
    fwd2 = np.block([[last.real, last.imag], [-last.imag, last.real]])
    inv2 = np.block([[last.real, -last.imag], [last.imag, last.real]])
    inv1 = np.concatenate([first.real.T, first.imag.T], axis=1) / total

    def stack_k(matrix):
        high, low = halves(matrix)
        return np.concatenate([high, low])

    high, low = halves(inv1)
    inv1 = np.concatenate([high, low], axis=1)
    turns = np.concatenate([turn.real, turn.imag], axis=1).astype(np.float32)
    return fwd1, stack_k(fwd2), stack_k(inv2), inv1, turns


def dot(left, right, dims=None):
    if dims is None:
        return jnp.dot(left, right, preferred_element_type=F32)
    return lax.dot_general(left, right, dims, preferred_element_type=F32)


def twice(value, axis):
    value = value.astype(BF16)
    return jnp.concatenate([value, value], axis=axis)


def spectrum(columns, fwd1, fwd2, turn_r, turn_i):
    joined = jnp.concatenate(columns, axis=1)
    stage = dot(fwd1, twice(joined, 0))
    rows = []
    for item in range(len(columns)):
        real = stage[:N1, N2 * item : N2 * (item + 1)]
        imag = stage[N1:, N2 * item : N2 * (item + 1)]
        turned = jnp.concatenate(
            [real * turn_r - imag * turn_i, real * turn_i + imag * turn_r], axis=1
        )
        rows.append(twice(turned, 1))
    done = dot(jnp.concatenate(rows, axis=0), fwd2)
    return [
        (done[N1 * i : N1 * (i + 1), :N2], done[N1 * i : N1 * (i + 1), N2:])
        for i in range(len(columns))
    ]


def positions(spectra, inv2, inv1, turn_r, turn_i):
    rows = []
    for real, imag in spectra:
        rows.append(twice(jnp.concatenate([real, imag], axis=1), 1))
    stage = dot(jnp.concatenate(rows, axis=0), inv2)
    columns = []
    for item in range(len(spectra)):
        real = stage[N1 * item : N1 * (item + 1), :N2]
        imag = stage[N1 * item : N1 * (item + 1), N2:]
        columns.append(
            jnp.concatenate(
                [real * turn_r + imag * turn_i, imag * turn_r - real * turn_i], axis=0
            )
        )
    done = dot(inv1, twice(jnp.concatenate(columns, axis=1), 0))
    return [done[:, N2 * i : N2 * (i + 1)] for i in range(len(spectra))]


class Exchange:
    def __init__(self, axis, size, source, target, sems):
        self.axis, self.size, self.source, self.target = axis, size, source, target
        self.send_sem, self.recv_sem = sems

    def copy(self, step):
        me = lax.axis_index(self.axis)
        peer = lax.rem(me + step, self.size)
        return pltpu.make_async_remote_copy(
            src_ref=self.source.at[peer],
            dst_ref=self.target.at[me],
            send_sem=self.send_sem.at[step],
            recv_sem=self.recv_sem.at[step],
            device_id={self.axis: peer},
            device_id_type=pl.DeviceIdType.MESH,
        )

    def start(self):
        @pl.loop(1, self.size)
        def _(step):
            self.copy(step).start()

        me = lax.axis_index(self.axis)
        self.target[me] = self.source[me]

    def wait(self):
        @pl.loop(1, self.size)
        def _(step):
            self.copy(step).wait()


def to_rows(value, scratch):
    channels, length = value.shape
    units = length // 128
    for u in range(units):
        scratch[pl.ds(u, channels, stride=units), :] = value[:, 128 * u : 128 * (u + 1)]
    return scratch[...]


def requests(rows, turned, ask_ref, place_ref):
    parts = ask_ref.shape[0]
    groups = rows.shape[0]
    owner = rows >> 15
    high = ((rows >> 8) & 127).astype(F32)
    low = (rows & 255).astype(F32) + 1.0
    each = lax.broadcasted_iota(I32, (parts, 128), 0)
    onehots = [(owner[b : b + 1, :] == each).astype(F32) for b in range(groups)]
    stacked = jnp.concatenate(onehots, axis=0).astype(BF16)
    size = groups * parts
    above = lax.broadcasted_iota(I32, (128, 128), 0) < lax.broadcasted_iota(I32, (128, 128), 1)
    within = dot(stacked, above.astype(BF16))
    totals = dot(stacked, jnp.ones((128, 128), BF16))
    to, of = lax.broadcasted_iota(I32, (size, size), 0), lax.broadcasted_iota(I32, (size, size), 1)
    earlier = ((to - of) > 0) & (lax.rem(to + size - of, parts) == 0)
    rank = within + dot(earlier.astype(BF16), totals.astype(BF16))
    target = lax.broadcasted_iota(I32, (128, 128), 0).astype(F32)
    asked = jnp.zeros((2 * parts, 128), F32)
    for b in range(groups):
        mine = jnp.sum(onehots[b] * rank[parts * b : parts * (b + 1)], axis=0, keepdims=True)
        at = (mine.astype(I32) + turned) & 127
        place_ref[b : b + 1, :] = owner[b : b + 1, :] * 128 + at
        ranks = (target == at.astype(F32)).astype(BF16)
        values = jnp.concatenate(
            [onehots[b] * high[b : b + 1, :], onehots[b] * low[b : b + 1, :]], axis=0
        )
        asked = asked + dot(values.astype(BF16), ranks, NT)
    asked = 256.0 * asked[:parts] + asked[parts:]
    for o in range(parts):
        ask_ref[o] = jnp.broadcast_to(asked[o : o + 1, :], (8, 128))


def packed(pieces):
    lane = lax.broadcasted_iota(I32, pieces[0].shape, 1)
    out = []
    for first in range(0, len(pieces), 4):
        p = pieces[first : first + 4]
        out += [jnp.where(lane < cut, p[i], p[i + 1]) for i, cut in enumerate((96, 64, 32))]
    return jnp.concatenate(out, axis=1)


def unpacked(joined):
    t = [joined[:, 128 * i : 128 * (i + 1)] for i in range(3)]
    lane = lax.broadcasted_iota(I32, t[0].shape, 1)
    return [t[0], jnp.where(lane < 96, t[1], t[0]), jnp.where(lane < 64, t[2], t[1]), t[2]]


def lists(asked):
    return asked >> LOW_BITS, asked & (LOW - 1)


def find_rows(asked, folded, picked, row_found, found_ref):
    channels = row_found.shape[0]
    highs = folded.shape[0] // channels
    high, low = lists(asked)
    span, group = 512, 32
    for chunk in range(high.shape[1] // span):
        cut = slice(span * chunk, span * (chunk + 1))
        onehot = lax.broadcasted_iota(I32, (LOW, span), 0) == low[:, cut]
        picked[...] = jnp.where(onehot, 1.0, 0.0).astype(BF16)
        row = jnp.broadcast_to(high[:, cut], (channels, span))

        def step(g, total):
            start = pl.multiple_of(g * group * channels, group * channels)
            all_high = dot(folded[pl.ds(start, group * channels), :], picked[...])
            for h in range(group):
                part = all_high[channels * h : channels * (h + 1)]
                total = total + jnp.where(row == g * group + h, part, 0.0)
            return total

        row_found[:, cut] = lax.fori_loop(
            0, highs // group, step, jnp.zeros((channels, span), F32)
        )
    for first in range(0, found_ref.shape[0], 4):
        pieces = unpacked(row_found[:, 96 * first : 96 * (first + 4)])
        for i, piece in enumerate(pieces):
            found_ref[first + i] = piece.astype(BF16)


def low_columns(asked, columns):
    high, low = lists(asked)
    for s in range(low.shape[1] // 128):
        lows = jnp.broadcast_to(low[:, 128 * s : 128 * (s + 1)], (128, 128)).astype(F32).T
        lows = jnp.concatenate([lows] * (LOW // 128), axis=1)
        onehot = lows == lax.broadcasted_iota(I32, (128, LOW), 1).astype(F32)
        columns[128 * s : 128 * (s + 1), :] = jnp.where(onehot, 1.0, 0.0).astype(BF16)


def add_rows(asked, values, columns, first, group, sums_ref):
    channels = values.shape[0]
    high, _ = lists(asked)
    row = jnp.broadcast_to(high.astype(F32).astype(BF16), values.shape)
    zero = jnp.zeros_like(values)
    rows = [jnp.where(row == jnp.asarray(first + h, BF16), values, zero) for h in range(group)]
    sums = dot(jnp.concatenate(rows, axis=0), columns[...])
    for h in range(group):
        sums_ref[:, LOW * h : LOW * (h + 1)] = sums[channels * h : channels * (h + 1)]


def step_body(
    seq, chan, filter_scale, score_scale,
    ids_ref, counts_ref, lanes_ref, signal_ref, taps_ref, gain_ref, *refs,
):
    later_hbm, refs = refs[:9], refs[9:]
    lag_ref, back, grad_gate_ref, values_ref, asked_ref, half_hbm = refs[:6]
    (
    data_s, data_r, ask_s, ask_r, conv_s, conv_r, found_s, found_r, enc_s, enc_r, embed_s, embed_r,
    negs_s, negs_r, slot_s, slot_r, gback_s, gback_r, out_s, out_r, res_s, res_r,
    place, flat, pre, spec, picked_rows, folded, picked, row_found, columns, sums, places,
    send_sems, recv_sems, local_sems, out_sem,
    *later,
    ) = refs[6:]
    item, fwd1, fwd2, inv2, inv1, turns, gate_ref, positive_ref, table = later
    channels, length = signal_ref.shape
    units = length // 128
    own = channels // seq
    groups = place.shape[0]

    def sems(i):
        return send_sems.at[i], recv_sems.at[i]

    data_x = Exchange("seq", seq, data_s, data_r, sems(0))
    ask_x = Exchange("seq", seq, ask_s, ask_r, sems(1))
    conv_x = Exchange("seq", seq, conv_s, conv_r, sems(2))
    found_x = Exchange("seq", seq, found_s, found_r, sems(3))
    enc_x = Exchange("chan", chan, enc_s, enc_r, sems(4))
    embed_x = Exchange("chan", chan, embed_s, embed_r, sems(5))
    negs_x = Exchange("chan", chan, negs_s, negs_r, sems(6))
    slot_x = Exchange("chan", chan, slot_s, slot_r, sems(7))
    gback_x = Exchange("seq", seq, gback_s, gback_r, sems(8))
    out_x = Exchange("seq", seq, out_s, out_r, sems(9))
    res_x = Exchange("seq", seq, res_s, res_r, sems(10))

    barrier = pltpu.get_barrier_semaphore()
    for axis, size in (("seq", seq), ("chan", chan)):
        me = lax.axis_index(axis)
        for step in range(1, size):
            pl.semaphore_signal(
                barrier,
                inc=1,
                device_id={axis: lax.rem(me + step, size)},
                device_id_type=pl.DeviceIdType.MESH,
            )
    loads = [
        pltpu.make_async_copy(s, t, local_sems.at[i])
        for i, (s, t) in enumerate(zip(later_hbm, later))
    ]
    for load in loads:
        load.start()

    for kind, ref in enumerate((signal_ref, taps_ref)):
        value = to_rows(ref[...].astype(F32), flat).astype(BF16)
        data_s[:, kind] = value.reshape(seq, own, units, 128)
    loads[0].wait()
    per = ids_ref.shape[1]

    @pl.loop(0, ids_ref.shape[0])
    def _(u):
        for j in range(per):
            picked_rows[pl.ds(u * per + j, 1), :] = item[pl.ds(ids_ref[u, j] >> 7, 1), :]

    pl.semaphore_wait(barrier, seq + chan - 2)
    data_x.start()

    rows = []
    ids = lanes_ref[...].astype(F32)
    lane_at = jnp.concatenate(
        [
            jnp.concatenate([ids[2 * b : 2 * b + 1], ids[2 * b + 1 : 2 * b + 2]], axis=1)
            for b in range(groups)
        ],
        axis=0,
    )
    lane_at = lane_at.astype(I32) & 127
    for b in range(groups):
        block = picked_rows[128 * b : 128 * (b + 1), :].astype(F32).T
        here = lax.broadcasted_iota(I32, (128, 128), 0) == lane_at[b : b + 1, :]
        rows.append(jnp.sum(jnp.where(here, block, 0.0), axis=0, keepdims=True))
    turned = (96 * lax.axis_index("seq")) & 127
    requests(jnp.concatenate(rows, axis=0).astype(I32), turned, ask_s, place)
    ask_x.start()

    for load in loads[1:]:
        load.wait()
    for h in range(table.shape[1] // LOW):
        folded[channels * h : channels * (h + 1), :] = table[:, LOW * h : LOW * (h + 1)]
    turn_r, turn_i = turns[:, :N2], turns[:, N2:]
    data_x.wait()
    spectra = spectrum(
        [data_r[:, kind, c].reshape(N1, N2) for kind in range(2) for c in range(own)],
        fwd1[...], fwd2[...], turn_r, turn_i,
    )
    for i, (real, imag) in enumerate(spectra):
        spec[i, 0] = real
        spec[i, 1] = imag
    products = []
    for c in range(own):
        (xr, xi), (hr, hi) = spectra[c], spectra[own + c]
        products.append((xr * hr - xi * hi, xr * hi + xi * hr))
    for c, value in enumerate(positions(products, inv2[...], inv1[...], turn_r, turn_i)):
        conv_s[:, c] = value.astype(BF16).reshape(seq, units, 128)
    conv_x.start()

    ask_x.wait()
    asked = packed([ask_r[s][0:1, :] for s in range(seq)]).astype(I32) - 1
    asked_ref[...] = jnp.broadcast_to(asked, asked_ref.shape)
    find_rows(asked, folded, picked, row_found, found_s)
    found_x.start()

    conv_x.wait()
    flat[...] = conv_r[...].reshape(channels * units, 128).astype(F32)
    square = lax.broadcasted_iota(I32, (channels, channels), 0) == lax.broadcasted_iota(
        I32, (channels, channels), 1
    )
    gain = jnp.sum(jnp.where(square, gain_ref[...], 0.0), axis=1, keepdims=True)
    tops = []
    for u in range(units):
        cut = slice(128 * u, 128 * (u + 1))
        conv = flat[pl.ds(u, channels, stride=units), :]
        value = filter_scale * conv + gain * signal_ref[:, cut].astype(F32)
        pre[:, cut] = value
        coded = (gate_ref[:, cut].astype(F32) * value).astype(BF16)
        enc_s[u // 2, :, 128 * (u % 2) : 128 * (u % 2 + 1)] = coded
        tops.append(
            jnp.sum(coded.astype(F32) * positive_ref[:, cut].astype(F32), axis=0, keepdims=True)
        )
    enc_x.start()
    for b in range(groups):
        top = jnp.concatenate(tops[2 * b : 2 * b + 2] + [jnp.zeros((14, 128), F32)], axis=0)
        embed_s[b, channels:, :] = top.astype(BF16)
        slot = lax.broadcasted_iota(I32, (seq * 128, 128), 0)
        places[b] = jnp.where(slot == place[b : b + 1, :], 1.0, 0.0).astype(BF16)

    found_x.wait()
    found = jnp.concatenate([found_r[o] for o in range(seq)], axis=1)
    for b in range(groups):
        embed_s[b, :channels, :] = dot(found, places[b]).astype(BF16)
    embed_x.start()

    low_columns(asked_ref[0:1, :], columns)
    enc_x.wait()
    coded = jnp.concatenate([enc_r[z] for z in range(chan)], axis=0)
    line = lax.broadcasted_iota(I32, (128, 128), 0)
    mine = 2 * lax.axis_index("chan")
    limit = jnp.where(line < 64, counts_ref[mine], 64 + counts_ref[mine + 1])
    embed_x.wait()
    embed = jnp.concatenate([embed_r[z, :channels, :] for z in range(chan)], axis=0)
    score = dot(embed, coded, TN)
    score = score_scale * jnp.where(line < 64, score[:, :128], score[:, 128:])
    weight = jnp.where(line < limit, 1.0 / (1.0 + jnp.exp(-score)), 0.0)
    weight = jnp.concatenate(
        [jnp.where(line < 64, weight, 0.0), jnp.where(line < 64, 0.0, weight)], axis=1
    ).astype(BF16)
    top = embed_r[0, channels:, :].astype(F32)
    for z in range(1, chan):
        top = top + embed_r[z, channels:, :].astype(F32)
    top = -1.0 / (1.0 + jnp.exp(score_scale * top))
    negs = dot(embed, weight).astype(BF16)
    for z in range(chan):
        negs_s[z, :channels, :] = negs[channels * z : channels * (z + 1)]
        negs_s[z, channels:, :128] = top.astype(BF16)
        negs_s[z, channels:, 128:] = top.astype(BF16)
    negs_x.start()
    slot = (score_scale * dot(coded, weight, NT)).astype(BF16)
    for z in range(chan):
        slot_s[z] = slot[channels * z : channels * (z + 1)]
    slot_x.start()

    negs_x.wait()
    for u in range(units):
        b, half = divmod(u, 2)
        cut, side = slice(128 * u, 128 * (u + 1)), slice(128 * half, 128 * (half + 1))
        top = negs_r[b, channels:, side].astype(F32)[half : half + 1, :]
        positive = positive_ref[:, cut].astype(F32)
        grad = score_scale * (top * positive + negs_r[b, :channels, side].astype(F32))
        grad_gate_ref[:, cut] = (grad * pre[:, cut]).astype(BF16)
        value = grad * gate_ref[:, cut].astype(F32)
        back[:, cut] = gain * value
        flat[pl.ds(u, channels, stride=units), :] = value
    gback_s[...] = flat[...].astype(BF16).reshape(gback_s.shape)
    gback_x.start()

    slot_x.wait()
    outgoing = jnp.zeros((channels, seq * 128), F32)
    for b in range(groups):
        outgoing = outgoing + dot(slot_r[b], places[b], NT)
    for o in range(seq):
        out_s[o] = outgoing[:, 128 * o : 128 * (o + 1)].astype(BF16)
    out_x.start()

    gback_x.wait()
    spectra = spectrum(
        [gback_r[:, c].reshape(N1, N2) for c in range(own)], fwd1[...], fwd2[...], turn_r, turn_i
    )
    products = []
    for kind in (1, 0):
        for c in range(own):
            (br, bi), at = spectra[c], kind * own + c
            sr, si = spec[at, 0], spec[at, 1]
            products.append((sr * br + si * bi, sr * bi - si * br))
    for i, value in enumerate(positions(products, inv2[...], inv1[...], turn_r, turn_i)):
        res_s[:, i // own, i % own] = value.astype(BF16).reshape(seq, units, 128)
    res_x.start()

    out_x.wait()
    values_ref[...] = packed([out_r[s].astype(F32) for s in range(seq)]).astype(BF16)
    half = sums.shape[1] // LOW
    add_rows(asked_ref[0:1, :], values_ref[...], columns, 0, half, sums)
    copy = pltpu.make_async_copy(sums, half_hbm, out_sem)
    copy.start()
    res_x.wait()
    lag_ref[...] = res_r[...]
    copy.wait()


def last_body(
    scale, lag_hbm, back_hbm, gate_hbm, values_ref, asked_ref, half_hbm,
    grad_signal_ref, grad_gate_ref, grad_filter_ref, grad_table_hbm,
    flat, columns, held, sums, lag_ref, back_ref, in_sems, out_sems,
):
    pieces, _, span = held.shape
    loads, copies = [], []
    for i in range(pieces):
        cut = slice(span * i, span * (i + 1))
        loads.append(pltpu.make_async_copy(half_hbm.at[:, cut], held.at[i], in_sems.at[i]))
        copies.append(
            pltpu.make_async_copy(held.at[i], grad_table_hbm.at[:, cut], out_sems.at[i])
        )
    for i in range(sums.shape[0]):
        start = span * pieces + sums.shape[2] * i
        copies.append(
            pltpu.make_async_copy(
                sums.at[i],
                grad_table_hbm.at[:, start : start + sums.shape[2]],
                out_sems.at[pieces + i],
            )
        )
    small = [
        pltpu.make_async_copy(lag_hbm, lag_ref, in_sems.at[pieces]),
        pltpu.make_async_copy(back_hbm, back_ref, in_sems.at[pieces + 1]),
        pltpu.make_async_copy(gate_hbm, grad_gate_ref, in_sems.at[pieces + 2]),
    ]
    for load in loads + small:
        load.start()
    asked = asked_ref[0:1, :]
    low_columns(asked, columns)
    for i in range(pieces):
        loads[i].wait()
        copies[i].start()
    group = sums.shape[2] // LOW
    for i in range(sums.shape[0]):
        first = span * pieces // LOW + group * i
        add_rows(asked, values_ref[...], columns, first, group, sums.at[i])
        copies[pieces + i].start()
    for load in small:
        load.wait()
    channels, length = back_ref.shape
    units = length // 128
    for kind, ref in enumerate((grad_signal_ref, grad_filter_ref)):
        flat[...] = lag_ref[:, kind].reshape(channels * units, 128).astype(F32)
        for u in range(units):
            cut = slice(128 * u, 128 * (u + 1))
            value = scale * flat[pl.ds(u, channels, stride=units), :]
            ref[:, cut] = value + back_ref[:, cut] if kind == 0 else value
    for copy in copies:
        copy.wait()


def local(
    seq, chan, signal, gate_values, filter_taps, skip_gain, positive, item_table, item_row,
    negative_ids, block_counts,
):
    channels, length = signal.shape
    units, own = length // 128, channels // seq
    rows_own = item_table.shape[1]
    slots = negative_ids.size
    groups = slots // 128
    first_highs = 40
    half = LOW * first_highs
    rest = rows_own - half
    tables = [jnp.asarray(t) for t in transform_tables()]
    later = [item_row.reshape(-1, 128), *tables, gate_values, positive, item_table]
    seq_pair = lambda *shape: [pltpu.VMEM((seq, *shape), BF16)] * 2
    scratch = [
        *seq_pair(2, own, units, 128),
        *[pltpu.VMEM((seq, 8, 128), F32)] * 2,
        *seq_pair(own, units, 128),
        *seq_pair(channels, 128),
        *[pltpu.VMEM((chan, channels, 256), BF16)] * 2,
        *[pltpu.VMEM((chan, channels + 16, 128), BF16)] * 2,
        *[pltpu.VMEM((chan, channels + 16, 256), BF16)] * 2,
        *[pltpu.VMEM((chan, channels, 128), BF16)] * 2,
        *seq_pair(own, units, 128),
        *seq_pair(channels, 128),
        *seq_pair(2, own, units, 128),
        pltpu.VMEM((groups, 128), I32),
        pltpu.VMEM((channels * units, 128), F32),
        pltpu.VMEM((channels, length), F32),
        pltpu.VMEM((2 * own, 2, N1, N2), F32),
        pltpu.VMEM((slots, 128), I32),
        pltpu.VMEM((channels * rows_own // LOW, LOW), BF16),
        pltpu.VMEM((LOW, 512), BF16),
        pltpu.VMEM((channels, seq * 96), F32),
        pltpu.VMEM((seq * 96, LOW), BF16),
        pltpu.VMEM((channels, half), F32),
        pltpu.VMEM((groups, seq * 128, 128), BF16),
        pltpu.SemaphoreType.DMA((11, seq)),
        pltpu.SemaphoreType.DMA((11, seq)),
        pltpu.SemaphoreType.DMA((len(later),)),
        pltpu.SemaphoreType.DMA,
        *[pltpu.VMEM(a.shape, a.dtype) for a in later],
    ]
    moved = pl.pallas_call(
        functools.partial(step_body, seq, chan, (seq * length) ** -0.5, C**-0.5),
        out_shape=[
            jax.ShapeDtypeStruct((seq, 2, own, units, 128), BF16),
            jax.ShapeDtypeStruct((channels, length), F32),
            jax.ShapeDtypeStruct((channels, length), BF16),
            jax.ShapeDtypeStruct((channels, seq * 96), BF16),
            jax.ShapeDtypeStruct((8, seq * 96), I32),
            jax.ShapeDtypeStruct((channels, half), F32),
        ],
        in_specs=[SMEM] * 2 + [VMEM] * 4 + [ANY] * len(later),
        out_specs=[VMEM] * 5 + [ANY],
        scratch_shapes=scratch,
        compiler_params=pltpu.CompilerParams(
            collective_id=1, has_side_effects=True, vmem_limit_bytes=LIMIT
        ),
        name="step",
    )(
        negative_ids, block_counts, negative_ids, signal, filter_taps,
        skip_gain.reshape(1, channels), *later,
    )
    return pl.pallas_call(
        functools.partial(last_body, (seq * length) ** -0.5),
        out_shape=[
            jax.ShapeDtypeStruct((channels, length), F32),
            jax.ShapeDtypeStruct((channels, length), BF16),
            jax.ShapeDtypeStruct((channels, length), F32),
            jax.ShapeDtypeStruct((channels, rows_own), F32),
        ],
        in_specs=[ANY] * 3 + [VMEM] * 2 + [ANY],
        out_specs=[VMEM] * 3 + [ANY],
        scratch_shapes=[
            pltpu.VMEM((channels * units, 128), F32),
            pltpu.VMEM((seq * 96, LOW), BF16),
            pltpu.VMEM((4, channels, half // 4), F32),
            pltpu.VMEM((2, channels, rest // 2), F32),
            pltpu.VMEM((seq, 2, own, units, 128), BF16),
            pltpu.VMEM((channels, length), F32),
            pltpu.SemaphoreType.DMA((7,)),
            pltpu.SemaphoreType.DMA((6,)),
        ],
        compiler_params=pltpu.CompilerParams(vmem_limit_bytes=LIMIT),
        name="last",
    )(*moved)


def solution(mesh):
    in_specs = (
        P("chan", "seq"),
        P("chan", "seq"),
        P("chan", "seq"),
        P("chan"),
        P("chan", "seq"),
        P("chan", "seq"),
        P(),
        P("seq", None),
        P("seq"),
    )
    out_specs = (P("chan", "seq"),) * 4
    body = functools.partial(local, mesh.shape["seq"], mesh.shape["chan"])
    return jax.shard_map(body, mesh=mesh, in_specs=in_specs, out_specs=out_specs, check_vma=False)
```

```python
import functools

import jax
import jax.numpy as jnp
import ml_dtypes
import numpy as np
from jax import lax
from jax.experimental import pallas as pl
from jax.experimental.pallas import tpu as pltpu
from jax.sharding import PartitionSpec as P

C = 256
F32, BF16, I32 = jnp.float32, jnp.bfloat16, jnp.int32
VMEM = pl.BlockSpec(memory_space=pltpu.VMEM)
SMEM = pl.BlockSpec(memory_space=pltpu.SMEM)
ANY = pl.BlockSpec(memory_space=pl.ANY)
N1, N2 = 256, 128
LOW_BITS = 9
LOW = 1 << LOW_BITS
LIMIT = 56 * 1024 * 1024
NT = (((1,), (1,)), ((), ()))
TN = (((0,), (0,)), ((), ()))


def halves(matrix):
    high = matrix.astype(ml_dtypes.bfloat16)
    return high, (matrix - high.astype(np.float64)).astype(ml_dtypes.bfloat16)


def transform_tables():
    total = N1 * N2
    k1, n1 = np.arange(N1) + 0.25, np.arange(N1)
    n2 = np.arange(N2)
    first = np.exp(-2j * np.pi * np.outer(k1, n1) / N1)
    turn = np.exp(-2j * np.pi * np.outer(k1, n2) / total)
    last = np.exp(-2j * np.pi * np.outer(n2, n2) / N2)
    fwd1 = np.concatenate(halves(np.concatenate([first.real, first.imag])), axis=1)
    fwd2 = np.block([[last.real, last.imag], [-last.imag, last.real]])
    inv2 = np.block([[last.real, -last.imag], [last.imag, last.real]])
    inv1 = np.concatenate([first.real.T, first.imag.T], axis=1) / total

    def stack_k(matrix):
        high, low = halves(matrix)
        return np.concatenate([high, low])

    high, low = halves(inv1)
    inv1 = np.concatenate([high, low], axis=1)
    turns = np.concatenate([turn.real, turn.imag], axis=1).astype(np.float32)
    return fwd1, stack_k(fwd2), stack_k(inv2), inv1, turns


def dot(left, right, dims=None):
    if dims is None:
        return jnp.dot(left, right, preferred_element_type=F32)
    return lax.dot_general(left, right, dims, preferred_element_type=F32)


def twice(value, axis):
    value = value.astype(BF16)
    return jnp.concatenate([value, value], axis=axis)


def spectrum(columns, fwd1, fwd2, turn_r, turn_i):
    joined = jnp.concatenate(columns, axis=1)
    stage = dot(fwd1, twice(joined, 0))
    rows = []
    for item in range(len(columns)):
        real = stage[:N1, N2 * item : N2 * (item + 1)]
        imag = stage[N1:, N2 * item : N2 * (item + 1)]
        turned = jnp.concatenate(
            [real * turn_r - imag * turn_i, real * turn_i + imag * turn_r], axis=1
        )
        rows.append(twice(turned, 1))
    done = dot(jnp.concatenate(rows, axis=0), fwd2)
    return [
        (done[N1 * i : N1 * (i + 1), :N2], done[N1 * i : N1 * (i + 1), N2:])
        for i in range(len(columns))
    ]


def positions(spectra, inv2, inv1, turn_r, turn_i):
    rows = []
    for real, imag in spectra:
        rows.append(twice(jnp.concatenate([real, imag], axis=1), 1))
    stage = dot(jnp.concatenate(rows, axis=0), inv2)
    columns = []
    for item in range(len(spectra)):
        real = stage[N1 * item : N1 * (item + 1), :N2]
        imag = stage[N1 * item : N1 * (item + 1), N2:]
        columns.append(
            jnp.concatenate(
                [real * turn_r + imag * turn_i, imag * turn_r - real * turn_i], axis=0
            )
        )
    done = dot(inv1, twice(jnp.concatenate(columns, axis=1), 0))
    return [done[:, N2 * i : N2 * (i + 1)] for i in range(len(spectra))]


class Exchange:
    def __init__(self, axis, size, source, target, sems):
        self.axis, self.size, self.source, self.target = axis, size, source, target
        self.send_sem, self.recv_sem = sems

    def copy(self, step):
        me = lax.axis_index(self.axis)
        peer = lax.rem(me + step, self.size)
        return pltpu.make_async_remote_copy(
            src_ref=self.source.at[peer],
            dst_ref=self.target.at[me],
            send_sem=self.send_sem.at[step],
            recv_sem=self.recv_sem.at[step],
            device_id={self.axis: peer},
            device_id_type=pl.DeviceIdType.MESH,
        )

    def start(self):
        @pl.loop(1, self.size)
        def _(step):
            self.copy(step).start()

        me = lax.axis_index(self.axis)
        self.target[me] = self.source[me]

    def wait(self):
        @pl.loop(1, self.size)
        def _(step):
            self.copy(step).wait()


def to_rows(value, scratch):
    channels, length = value.shape
    units = length // 128
    for u in range(units):
        scratch[pl.ds(u, channels, stride=units), :] = value[:, 128 * u : 128 * (u + 1)]
    return scratch[...]


def requests(rows, turned, ask_ref, place_ref):
    parts = ask_ref.shape[0]
    groups = rows.shape[0]
    owner = rows >> 15
    high = ((rows >> 8) & 127).astype(F32)
    low = (rows & 255).astype(F32) + 1.0
    each = lax.broadcasted_iota(I32, (parts, 128), 0)
    onehots = [(owner[b : b + 1, :] == each).astype(F32) for b in range(groups)]
    stacked = jnp.concatenate(onehots, axis=0).astype(BF16)
    size = groups * parts
    above = lax.broadcasted_iota(I32, (128, 128), 0) < lax.broadcasted_iota(I32, (128, 128), 1)
    within = dot(stacked, above.astype(BF16))
    totals = dot(stacked, jnp.ones((128, 128), BF16))
    to, of = lax.broadcasted_iota(I32, (size, size), 0), lax.broadcasted_iota(I32, (size, size), 1)
    earlier = ((to - of) > 0) & (lax.rem(to + size - of, parts) == 0)
    rank = within + dot(earlier.astype(BF16), totals.astype(BF16))
    target = lax.broadcasted_iota(I32, (128, 128), 0).astype(F32)
    asked = jnp.zeros((2 * parts, 128), F32)
    for b in range(groups):
        mine = jnp.sum(onehots[b] * rank[parts * b : parts * (b + 1)], axis=0, keepdims=True)
        at = (mine.astype(I32) + turned) & 127
        place_ref[b : b + 1, :] = owner[b : b + 1, :] * 128 + at
        ranks = (target == at.astype(F32)).astype(BF16)
        values = jnp.concatenate(
            [onehots[b] * high[b : b + 1, :], onehots[b] * low[b : b + 1, :]], axis=0
        )
        asked = asked + dot(values.astype(BF16), ranks, NT)
    asked = 256.0 * asked[:parts] + asked[parts:]
    for o in range(parts):
        ask_ref[o] = jnp.broadcast_to(asked[o : o + 1, :], (8, 128))


def packed(pieces):
    lane = lax.broadcasted_iota(I32, pieces[0].shape, 1)
    out = []
    for first in range(0, len(pieces), 4):
        p = pieces[first : first + 4]
        out += [jnp.where(lane < cut, p[i], p[i + 1]) for i, cut in enumerate((96, 64, 32))]
    return jnp.concatenate(out, axis=1)


def unpacked(joined):
    t = [joined[:, 128 * i : 128 * (i + 1)] for i in range(3)]
    lane = lax.broadcasted_iota(I32, t[0].shape, 1)
    return [t[0], jnp.where(lane < 96, t[1], t[0]), jnp.where(lane < 64, t[2], t[1]), t[2]]


def lists(asked):
    return asked >> LOW_BITS, asked & (LOW - 1)


def find_rows(asked, folded, picked, row_found, found_ref):
    channels = row_found.shape[0]
    highs = folded.shape[0] // channels
    high, low = lists(asked)
    span, group = 512, 32
    for chunk in range(high.shape[1] // span):
        cut = slice(span * chunk, span * (chunk + 1))
        onehot = lax.broadcasted_iota(I32, (LOW, span), 0) == low[:, cut]
        picked[...] = jnp.where(onehot, 1.0, 0.0).astype(BF16)
        row = jnp.broadcast_to(high[:, cut], (channels, span))

        def step(g, total):
            start = pl.multiple_of(g * group * channels, group * channels)
            all_high = dot(folded[pl.ds(start, group * channels), :], picked[...])
            for h in range(group):
                part = all_high[channels * h : channels * (h + 1)]
                total = total + jnp.where(row == g * group + h, part, 0.0)
            return total

        row_found[:, cut] = lax.fori_loop(
            0, highs // group, step, jnp.zeros((channels, span), F32)
        )
    for first in range(0, found_ref.shape[0], 4):
        pieces = unpacked(row_found[:, 96 * first : 96 * (first + 4)])
        for i, piece in enumerate(pieces):
            found_ref[first + i] = piece.astype(BF16)


def low_columns(asked, columns):
    high, low = lists(asked)
    for s in range(low.shape[1] // 128):
        lows = jnp.broadcast_to(low[:, 128 * s : 128 * (s + 1)], (128, 128)).astype(F32).T
        lows = jnp.concatenate([lows] * (LOW // 128), axis=1)
        onehot = lows == lax.broadcasted_iota(I32, (128, LOW), 1).astype(F32)
        columns[128 * s : 128 * (s + 1), :] = jnp.where(onehot, 1.0, 0.0).astype(BF16)


def add_rows(asked, values, columns, first, group, sums_ref):
    channels = values.shape[0]
    high, _ = lists(asked)
    row = jnp.broadcast_to(high.astype(F32).astype(BF16), values.shape)
    zero = jnp.zeros_like(values)
    rows = [jnp.where(row == jnp.asarray(first + h, BF16), values, zero) for h in range(group)]
    sums = dot(jnp.concatenate(rows, axis=0), columns[...])
    for h in range(group):
        sums_ref[:, LOW * h : LOW * (h + 1)] = sums[channels * h : channels * (h + 1)]


def step_body(
    seq, chan, filter_scale, score_scale,
    ids_ref, counts_ref, *refs,
):
    later_hbm, refs = refs[:13], refs[13:]
    *moved_hbm, half_hbm = refs[:6]
    (
    data_s, data_r, ask_s, ask_r, conv_s, conv_r, found_s, found_r, enc_s, enc_r, embed_s, embed_r,
    negs_s, negs_r, slot_s, slot_r, gback_s, gback_r, out_s, out_r, res_s, res_r,
    place, flat, pre, spec, picked_rows, folded, picked, row_found, columns, sums, places,
    send_sems, recv_sems, local_sems, out_sems, back, gate_grad, values_ref, asked_ref,
    *later,
    ) = refs[6:]
    (
        signal_ref, taps_ref, item, lanes_ref, gain_ref, fwd1, fwd2, inv2, inv1, turns,
        gate_ref, positive_ref, table,
    ) = later
    channels, length = signal_ref.shape
    units = length // 128
    own = channels // seq
    groups = place.shape[0]

    def sems(i):
        return send_sems.at[i], recv_sems.at[i]

    data_x = Exchange("seq", seq, data_s, data_r, sems(0))
    ask_x = Exchange("seq", seq, ask_s, ask_r, sems(1))
    conv_x = Exchange("seq", seq, conv_s, conv_r, sems(2))
    found_x = Exchange("seq", seq, found_s, found_r, sems(3))
    enc_x = Exchange("chan", chan, enc_s, enc_r, sems(4))
    embed_x = Exchange("chan", chan, embed_s, embed_r, sems(5))
    negs_x = Exchange("chan", chan, negs_s, negs_r, sems(6))
    slot_x = Exchange("chan", chan, slot_s, slot_r, sems(7))
    gback_x = Exchange("seq", seq, gback_s, gback_r, sems(8))
    out_x = Exchange("seq", seq, out_s, out_r, sems(9))
    res_x = Exchange("seq", seq, res_s, res_r, sems(10))

    barrier = pltpu.get_barrier_semaphore()
    for axis, size in (("seq", seq), ("chan", chan)):
        me = lax.axis_index(axis)
        for step in range(1, size):
            pl.semaphore_signal(
                barrier,
                inc=1,
                device_id={axis: lax.rem(me + step, size)},
                device_id_type=pl.DeviceIdType.MESH,
            )
    loads = [
        pltpu.make_async_copy(s, t, local_sems.at[i])
        for i, (s, t) in enumerate(zip(later_hbm, later))
    ]
    for load in loads:
        load.start()

    outs = [
        pltpu.make_async_copy(s, t, out_sems.at[i])
        for i, (s, t) in enumerate(zip((res_r, back, gate_grad, values_ref, asked_ref), moved_hbm))
    ]
    for kind, ref in enumerate((signal_ref, taps_ref)):
        loads[kind].wait()
        value = to_rows(ref[...].astype(F32), flat).astype(BF16)
        data_s[:, kind] = value.reshape(seq, own, units, 128)
    loads[2].wait()
    per = ids_ref.shape[1]

    @pl.loop(0, ids_ref.shape[0])
    def _(u):
        for j in range(per):
            picked_rows[pl.ds(u * per + j, 1), :] = item[pl.ds(ids_ref[u, j] >> 7, 1), :]

    pl.semaphore_wait(barrier, seq + chan - 2)
    data_x.start()

    rows = []
    loads[3].wait()
    ids = lanes_ref[...].astype(F32)
    lane_at = jnp.concatenate(
        [
            jnp.concatenate([ids[2 * b : 2 * b + 1], ids[2 * b + 1 : 2 * b + 2]], axis=1)
            for b in range(groups)
        ],
        axis=0,
    )
    lane_at = lane_at.astype(I32) & 127
    for b in range(groups):
        block = picked_rows[128 * b : 128 * (b + 1), :].astype(F32).T
        here = lax.broadcasted_iota(I32, (128, 128), 0) == lane_at[b : b + 1, :]
        rows.append(jnp.sum(jnp.where(here, block, 0.0), axis=0, keepdims=True))
    turned = (96 * lax.axis_index("seq")) & 127
    requests(jnp.concatenate(rows, axis=0).astype(I32), turned, ask_s, place)
    ask_x.start()

    for load in loads[4:]:
        load.wait()
    for h in range(table.shape[1] // LOW):
        folded[channels * h : channels * (h + 1), :] = table[:, LOW * h : LOW * (h + 1)]
    turn_r, turn_i = turns[:, :N2], turns[:, N2:]
    data_x.wait()
    spectra = spectrum(
        [data_r[:, kind, c].reshape(N1, N2) for kind in range(2) for c in range(own)],
        fwd1[...], fwd2[...], turn_r, turn_i,
    )
    for i, (real, imag) in enumerate(spectra):
        spec[i, 0] = real
        spec[i, 1] = imag
    products = []
    for c in range(own):
        (xr, xi), (hr, hi) = spectra[c], spectra[own + c]
        products.append((xr * hr - xi * hi, xr * hi + xi * hr))
    for c, value in enumerate(positions(products, inv2[...], inv1[...], turn_r, turn_i)):
        conv_s[:, c] = value.astype(BF16).reshape(seq, units, 128)
    conv_x.start()

    ask_x.wait()
    asked = packed([ask_r[s][0:1, :] for s in range(seq)]).astype(I32) - 1
    asked_ref[...] = jnp.broadcast_to(asked, asked_ref.shape)
    outs[4].start()
    find_rows(asked, folded, picked, row_found, found_s)
    found_x.start()

    conv_x.wait()
    flat[...] = conv_r[...].reshape(channels * units, 128).astype(F32)
    square = lax.broadcasted_iota(I32, (channels, channels), 0) == lax.broadcasted_iota(
        I32, (channels, channels), 1
    )
    gain = jnp.sum(jnp.where(square, gain_ref[...], 0.0), axis=1, keepdims=True)
    tops = []
    for u in range(units):
        cut = slice(128 * u, 128 * (u + 1))
        conv = flat[pl.ds(u, channels, stride=units), :]
        value = filter_scale * conv + gain * signal_ref[:, cut].astype(F32)
        pre[:, cut] = value
        coded = (gate_ref[:, cut].astype(F32) * value).astype(BF16)
        enc_s[u // 2, :, 128 * (u % 2) : 128 * (u % 2 + 1)] = coded
        tops.append(
            jnp.sum(coded.astype(F32) * positive_ref[:, cut].astype(F32), axis=0, keepdims=True)
        )
    enc_x.start()
    for b in range(groups):
        top = jnp.concatenate(tops[2 * b : 2 * b + 2] + [jnp.zeros((14, 128), F32)], axis=0)
        embed_s[b, channels:, :] = top.astype(BF16)
        slot = lax.broadcasted_iota(I32, (seq * 128, 128), 0)
        places[b] = jnp.where(slot == place[b : b + 1, :], 1.0, 0.0).astype(BF16)

    found_x.wait()
    found = jnp.concatenate([found_r[o] for o in range(seq)], axis=1)
    for b in range(groups):
        embed_s[b, :channels, :] = dot(found, places[b]).astype(BF16)
    embed_x.start()

    low_columns(asked_ref[0:1, :], columns)
    enc_x.wait()
    coded = jnp.concatenate([enc_r[z] for z in range(chan)], axis=0)
    line = lax.broadcasted_iota(I32, (128, 128), 0)
    mine = 2 * lax.axis_index("chan")
    limit = jnp.where(line < 64, counts_ref[mine], 64 + counts_ref[mine + 1])
    embed_x.wait()
    embed = jnp.concatenate([embed_r[z, :channels, :] for z in range(chan)], axis=0)
    score = dot(embed, coded, TN)
    score = score_scale * jnp.where(line < 64, score[:, :128], score[:, 128:])
    weight = jnp.where(line < limit, 1.0 / (1.0 + jnp.exp(-score)), 0.0)
    weight = jnp.concatenate(
        [jnp.where(line < 64, weight, 0.0), jnp.where(line < 64, 0.0, weight)], axis=1
    ).astype(BF16)
    top = embed_r[0, channels:, :].astype(F32)
    for z in range(1, chan):
        top = top + embed_r[z, channels:, :].astype(F32)
    top = -1.0 / (1.0 + jnp.exp(score_scale * top))
    negs = dot(embed, weight).astype(BF16)
    for z in range(chan):
        negs_s[z, :channels, :] = negs[channels * z : channels * (z + 1)]
        negs_s[z, channels:, :128] = top.astype(BF16)
        negs_s[z, channels:, 128:] = top.astype(BF16)
    negs_x.start()
    slot = (score_scale * dot(coded, weight, NT)).astype(BF16)
    for z in range(chan):
        slot_s[z] = slot[channels * z : channels * (z + 1)]
    slot_x.start()

    negs_x.wait()
    for u in range(units):
        b, half = divmod(u, 2)
        cut, side = slice(128 * u, 128 * (u + 1)), slice(128 * half, 128 * (half + 1))
        top = negs_r[b, channels:, side].astype(F32)[half : half + 1, :]
        positive = positive_ref[:, cut].astype(F32)
        grad = score_scale * (top * positive + negs_r[b, :channels, side].astype(F32))
        gate_grad[:, cut] = (grad * pre[:, cut]).astype(BF16)
        value = grad * gate_ref[:, cut].astype(F32)
        back[:, cut] = gain * value
        flat[pl.ds(u, channels, stride=units), :] = value
    gback_s[...] = flat[...].astype(BF16).reshape(gback_s.shape)
    gback_x.start()
    outs[1].start()
    outs[2].start()

    slot_x.wait()
    outgoing = jnp.zeros((channels, seq * 128), F32)
    for b in range(groups):
        outgoing = outgoing + dot(slot_r[b], places[b], NT)
    for o in range(seq):
        out_s[o] = outgoing[:, 128 * o : 128 * (o + 1)].astype(BF16)
    out_x.start()

    gback_x.wait()
    spectra = spectrum(
        [gback_r[:, c].reshape(N1, N2) for c in range(own)], fwd1[...], fwd2[...], turn_r, turn_i
    )
    products = []
    for kind in (1, 0):
        for c in range(own):
            (br, bi), at = spectra[c], kind * own + c
            sr, si = spec[at, 0], spec[at, 1]
            products.append((sr * br + si * bi, sr * bi - si * br))
    for i, value in enumerate(positions(products, inv2[...], inv1[...], turn_r, turn_i)):
        res_s[:, i // own, i % own] = value.astype(BF16).reshape(seq, units, 128)
    res_x.start()

    out_x.wait()
    values_ref[...] = packed([out_r[s].astype(F32) for s in range(seq)]).astype(BF16)
    outs[3].start()
    groups, _, span = sums.shape
    halves = [
        pltpu.make_async_copy(
            sums.at[g], half_hbm.at[:, span * g : span * (g + 1)], out_sems.at[len(outs) + g]
        )
        for g in range(groups)
    ]
    group = span // LOW
    for g in range(groups):
        add_rows(asked_ref[0:1, :], values_ref[...], columns, group * g, group, sums.at[g])
        halves[g].start()
    res_x.wait()
    outs[0].start()
    for copy in outs + halves:
        copy.wait()


def last_body(
    scale, lag_hbm, back_hbm, gate_hbm, values_hbm, asked_hbm, half_hbm,
    grad_signal_hbm, grad_gate_hbm, grad_filter_hbm, grad_table_hbm,
    flat, columns, held, sums, lag_ref, back_ref, gate_ref, values_ref, asked_ref, results,
    in_sems, out_sems,
):
    pieces, _, span = held.shape
    loads, copies = [], []
    for i in range(pieces):
        cut = slice(span * i, span * (i + 1))
        loads.append(pltpu.make_async_copy(half_hbm.at[:, cut], held.at[i], in_sems.at[i]))
        copies.append(
            pltpu.make_async_copy(held.at[i], grad_table_hbm.at[:, cut], out_sems.at[i])
        )
    for i in range(sums.shape[0]):
        start = span * pieces + sums.shape[2] * i
        copies.append(
            pltpu.make_async_copy(
                sums.at[i],
                grad_table_hbm.at[:, start : start + sums.shape[2]],
                out_sems.at[pieces + i],
            )
        )
    small = [
        pltpu.make_async_copy(source, target, in_sems.at[pieces + i])
        for i, (source, target) in enumerate(
            (
                (asked_hbm, asked_ref),
                (values_hbm, values_ref),
                (gate_hbm, gate_ref),
                (lag_hbm, lag_ref),
                (back_hbm, back_ref),
            )
        )
    ]
    for load in small[:2] + loads + small[2:]:
        load.start()
    ends = [
        pltpu.make_async_copy(source, target, out_sems.at[len(copies) + i])
        for i, (source, target) in enumerate(
            (
                (results.at[0], grad_signal_hbm),
                (results.at[1], grad_filter_hbm),
                (gate_ref, grad_gate_hbm),
            )
        )
    ]
    small[0].wait()
    asked = asked_ref[0:1, :]
    low_columns(asked, columns)
    for i in range(pieces):
        loads[i].wait()
        copies[i].start()
    small[1].wait()
    group = sums.shape[2] // LOW
    for i in range(sums.shape[0]):
        first = span * pieces // LOW + group * i
        add_rows(asked, values_ref[...], columns, first, group, sums.at[i])
        copies[pieces + i].start()
    for load in small[2:]:
        load.wait()
    ends[2].start()
    channels, length = back_ref.shape
    units = length // 128
    for kind in range(2):
        flat[...] = lag_ref[:, kind].reshape(channels * units, 128).astype(F32)
        for u in range(units):
            cut = slice(128 * u, 128 * (u + 1))
            value = scale * flat[pl.ds(u, channels, stride=units), :]
            results[kind, :, cut] = value + back_ref[:, cut] if kind == 0 else value
        ends[kind].start()
    for copy in copies + ends:
        copy.wait()


def local(
    seq, chan, signal, gate_values, filter_taps, skip_gain, positive, item_table, item_row,
    negative_ids, block_counts,
):
    channels, length = signal.shape
    units, own = length // 128, channels // seq
    rows_own = item_table.shape[1]
    slots = negative_ids.size
    groups = slots // 128
    first_highs = 48
    half = LOW * first_highs
    rest = rows_own - half
    tables = [jnp.asarray(t) for t in transform_tables()]
    later = [
        signal, filter_taps, item_row.reshape(-1, 128), negative_ids, skip_gain.reshape(1, channels),
        *tables, gate_values, positive, item_table,
    ]
    seq_pair = lambda *shape: [pltpu.VMEM((seq, *shape), BF16)] * 2
    scratch = [
        *seq_pair(2, own, units, 128),
        *[pltpu.VMEM((seq, 8, 128), F32)] * 2,
        *seq_pair(own, units, 128),
        *seq_pair(channels, 128),
        *[pltpu.VMEM((chan, channels, 256), BF16)] * 2,
        *[pltpu.VMEM((chan, channels + 16, 128), BF16)] * 2,
        *[pltpu.VMEM((chan, channels + 16, 256), BF16)] * 2,
        *[pltpu.VMEM((chan, channels, 128), BF16)] * 2,
        *seq_pair(own, units, 128),
        *seq_pair(channels, 128),
        *seq_pair(2, own, units, 128),
        pltpu.VMEM((groups, 128), I32),
        pltpu.VMEM((channels * units, 128), F32),
        pltpu.VMEM((channels, length), F32),
        pltpu.VMEM((2 * own, 2, N1, N2), F32),
        pltpu.VMEM((slots, 128), I32),
        pltpu.VMEM((channels * rows_own // LOW, LOW), BF16),
        pltpu.VMEM((LOW, 512), BF16),
        pltpu.VMEM((channels, seq * 96), F32),
        pltpu.VMEM((seq * 96, LOW), BF16),
        pltpu.VMEM((3, channels, half // 3), F32),
        pltpu.VMEM((groups, seq * 128, 128), BF16),
        pltpu.SemaphoreType.DMA((11, seq)),
        pltpu.SemaphoreType.DMA((11, seq)),
        pltpu.SemaphoreType.DMA((len(later),)),
        pltpu.SemaphoreType.DMA((8,)),
        pltpu.VMEM((channels, length), F32),
        pltpu.VMEM((channels, length), BF16),
        pltpu.VMEM((channels, seq * 96), BF16),
        pltpu.VMEM((8, seq * 96), I32),
        *[pltpu.VMEM(a.shape, a.dtype) for a in later],
    ]
    moved = pl.pallas_call(
        functools.partial(step_body, seq, chan, (seq * length) ** -0.5, C**-0.5),
        out_shape=[
            jax.ShapeDtypeStruct((seq, 2, own, units, 128), BF16),
            jax.ShapeDtypeStruct((channels, length), F32),
            jax.ShapeDtypeStruct((channels, length), BF16),
            jax.ShapeDtypeStruct((channels, seq * 96), BF16),
            jax.ShapeDtypeStruct((8, seq * 96), I32),
            jax.ShapeDtypeStruct((channels, half), F32),
        ],
        in_specs=[SMEM] * 2 + [ANY] * len(later),
        out_specs=[ANY] * 6,
        scratch_shapes=scratch,
        compiler_params=pltpu.CompilerParams(
            collective_id=1, has_side_effects=True, vmem_limit_bytes=LIMIT
        ),
        name="step",
    )(negative_ids, block_counts, *later)
    return pl.pallas_call(
        functools.partial(last_body, (seq * length) ** -0.5),
        out_shape=[
            jax.ShapeDtypeStruct((channels, length), F32),
            jax.ShapeDtypeStruct((channels, length), BF16),
            jax.ShapeDtypeStruct((channels, length), F32),
            jax.ShapeDtypeStruct((channels, rows_own), F32),
        ],
        in_specs=[ANY] * 6,
        out_specs=[ANY] * 4,
        scratch_shapes=[
            pltpu.VMEM((channels * units, 128), F32),
            pltpu.VMEM((seq * 96, LOW), BF16),
            pltpu.VMEM((4, channels, half // 4), F32),
            pltpu.VMEM((2, channels, rest // 2), F32),
            pltpu.VMEM((seq, 2, own, units, 128), BF16),
            pltpu.VMEM((channels, length), F32),
            pltpu.VMEM((channels, length), BF16),
            pltpu.VMEM((channels, seq * 96), BF16),
            pltpu.VMEM((8, seq * 96), I32),
            pltpu.VMEM((2, channels, length), F32),
            pltpu.SemaphoreType.DMA((9,)),
            pltpu.SemaphoreType.DMA((9,)),
        ],
        compiler_params=pltpu.CompilerParams(vmem_limit_bytes=LIMIT),
        name="last",
    )(*moved)


def solution(mesh):
    in_specs = (
        P("chan", "seq"),
        P("chan", "seq"),
        P("chan", "seq"),
        P("chan"),
        P("chan", "seq"),
        P("chan", "seq"),
        P(),
        P("seq", None),
        P("seq"),
    )
    out_specs = (P("chan", "seq"),) * 4
    body = functools.partial(local, mesh.shape["seq"], mesh.shape["chan"])
    return jax.shard_map(body, mesh=mesh, in_specs=in_specs, out_specs=out_specs, check_vma=False)
```

```python
import functools

import jax
import jax.numpy as jnp
import ml_dtypes
import numpy as np
from jax import lax
from jax.experimental import pallas as pl
from jax.experimental.pallas import tpu as pltpu
from jax.sharding import PartitionSpec as P

C = 256
F32, BF16, I32 = jnp.float32, jnp.bfloat16, jnp.int32
VMEM = pl.BlockSpec(memory_space=pltpu.VMEM)
SMEM = pl.BlockSpec(memory_space=pltpu.SMEM)
ANY = pl.BlockSpec(memory_space=pl.ANY)
N1, N2 = 256, 128
LOW_BITS = 9
LOW = 1 << LOW_BITS
LIMIT = 56 * 1024 * 1024
NT = (((1,), (1,)), ((), ()))
TN = (((0,), (0,)), ((), ()))


def halves(matrix):
    high = matrix.astype(ml_dtypes.bfloat16)
    return high, (matrix - high.astype(np.float64)).astype(ml_dtypes.bfloat16)


def transform_tables():
    total = N1 * N2
    k1, n1 = np.arange(N1) + 0.25, np.arange(N1)
    n2 = np.arange(N2)
    first = np.exp(-2j * np.pi * np.outer(k1, n1) / N1)
    turn = np.exp(-2j * np.pi * np.outer(k1, n2) / total)
    last = np.exp(-2j * np.pi * np.outer(n2, n2) / N2)
    fwd1 = np.concatenate(halves(np.concatenate([first.real, first.imag])), axis=1)
    fwd2 = np.block([[last.real, last.imag], [-last.imag, last.real]])
    inv2 = np.block([[last.real, -last.imag], [last.imag, last.real]])
    inv1 = np.concatenate([first.real.T, first.imag.T], axis=1) / total

    def stack_k(matrix):
        high, low = halves(matrix)
        return np.concatenate([high, low])

    high, low = halves(inv1)
    inv1 = np.concatenate([high, low], axis=1)
    turns = np.concatenate([turn.real, turn.imag], axis=1).astype(np.float32)
    return fwd1, stack_k(fwd2), stack_k(inv2), inv1, turns


def dot(left, right, dims=None):
    if dims is None:
        return jnp.dot(left, right, preferred_element_type=F32)
    return lax.dot_general(left, right, dims, preferred_element_type=F32)


def twice(value, axis):
    value = value.astype(BF16)
    return jnp.concatenate([value, value], axis=axis)


def spectrum(columns, fwd1, fwd2, turn_r, turn_i):
    joined = jnp.concatenate(columns, axis=1)
    stage = dot(fwd1, twice(joined, 0))
    rows = []
    for item in range(len(columns)):
        real = stage[:N1, N2 * item : N2 * (item + 1)]
        imag = stage[N1:, N2 * item : N2 * (item + 1)]
        turned = jnp.concatenate(
            [real * turn_r - imag * turn_i, real * turn_i + imag * turn_r], axis=1
        )
        rows.append(twice(turned, 1))
    done = dot(jnp.concatenate(rows, axis=0), fwd2)
    return [
        (done[N1 * i : N1 * (i + 1), :N2], done[N1 * i : N1 * (i + 1), N2:])
        for i in range(len(columns))
    ]


def positions(spectra, inv2, inv1, turn_r, turn_i):
    rows = []
    for real, imag in spectra:
        rows.append(twice(jnp.concatenate([real, imag], axis=1), 1))
    stage = dot(jnp.concatenate(rows, axis=0), inv2)
    columns = []
    for item in range(len(spectra)):
        real = stage[N1 * item : N1 * (item + 1), :N2]
        imag = stage[N1 * item : N1 * (item + 1), N2:]
        columns.append(
            jnp.concatenate(
                [real * turn_r + imag * turn_i, imag * turn_r - real * turn_i], axis=0
            )
        )
    done = dot(inv1, twice(jnp.concatenate(columns, axis=1), 0))
    return [done[:, N2 * i : N2 * (i + 1)] for i in range(len(spectra))]


class Exchange:
    def __init__(self, axis, size, source, target, sems):
        self.axis, self.size, self.source, self.target = axis, size, source, target
        self.send_sem, self.recv_sem = sems

    def copy(self, step):
        me = lax.axis_index(self.axis)
        peer = lax.rem(me + step, self.size)
        return pltpu.make_async_remote_copy(
            src_ref=self.source.at[peer],
            dst_ref=self.target.at[me],
            send_sem=self.send_sem,
            recv_sem=self.recv_sem,
            device_id={self.axis: peer},
            device_id_type=pl.DeviceIdType.MESH,
        )

    def start(self):
        @pl.loop(1, self.size)
        def _(step):
            self.copy(step).start()

        me = lax.axis_index(self.axis)
        self.target[me] = self.source[me]

    def wait(self):
        me = lax.axis_index(self.axis)
        pltpu.make_async_remote_copy(
            src_ref=self.source.at[pl.ds(0, self.size - 1)],
            dst_ref=self.target.at[pl.ds(0, self.size - 1)],
            send_sem=self.send_sem,
            recv_sem=self.recv_sem,
            device_id={self.axis: lax.rem(me + 1, self.size)},
            device_id_type=pl.DeviceIdType.MESH,
        ).wait()


def to_rows(value, scratch):
    channels, length = value.shape
    units = length // 128
    for u in range(units):
        scratch[pl.ds(u, channels, stride=units), :] = value[:, 128 * u : 128 * (u + 1)]
    return scratch[...]


def requests(rows, turned, ask_ref, place_ref):
    parts = ask_ref.shape[0]
    groups = rows.shape[0]
    owner = rows >> 15
    high = ((rows >> 8) & 127).astype(F32)
    low = (rows & 255).astype(F32) + 1.0
    each = lax.broadcasted_iota(I32, (parts, 128), 0)
    onehots = [(owner[b : b + 1, :] == each).astype(F32) for b in range(groups)]
    stacked = jnp.concatenate(onehots, axis=0).astype(BF16)
    size = groups * parts
    above = lax.broadcasted_iota(I32, (128, 128), 0) < lax.broadcasted_iota(I32, (128, 128), 1)
    within = dot(stacked, above.astype(BF16))
    totals = dot(stacked, jnp.ones((128, 128), BF16))
    to, of = lax.broadcasted_iota(I32, (size, size), 0), lax.broadcasted_iota(I32, (size, size), 1)
    earlier = ((to - of) > 0) & (lax.rem(to + size - of, parts) == 0)
    rank = within + dot(earlier.astype(BF16), totals.astype(BF16))
    target = lax.broadcasted_iota(I32, (128, 128), 0).astype(F32)
    asked = jnp.zeros((2 * parts, 128), F32)
    for b in range(groups):
        mine = jnp.sum(onehots[b] * rank[parts * b : parts * (b + 1)], axis=0, keepdims=True)
        at = (mine.astype(I32) + turned) & 127
        place_ref[b : b + 1, :] = owner[b : b + 1, :] * 128 + at
        ranks = (target == at.astype(F32)).astype(BF16)
        values = jnp.concatenate(
            [onehots[b] * high[b : b + 1, :], onehots[b] * low[b : b + 1, :]], axis=0
        )
        asked = asked + dot(values.astype(BF16), ranks, NT)
    asked = 256.0 * asked[:parts] + asked[parts:]
    for o in range(parts):
        ask_ref[o] = jnp.broadcast_to(asked[o : o + 1, :], (8, 128))


def packed(pieces):
    lane = lax.broadcasted_iota(I32, pieces[0].shape, 1)
    out = []
    for first in range(0, len(pieces), 4):
        p = pieces[first : first + 4]
        out += [jnp.where(lane < cut, p[i], p[i + 1]) for i, cut in enumerate((96, 64, 32))]
    return jnp.concatenate(out, axis=1)


def unpacked(joined):
    t = [joined[:, 128 * i : 128 * (i + 1)] for i in range(3)]
    lane = lax.broadcasted_iota(I32, t[0].shape, 1)
    return [t[0], jnp.where(lane < 96, t[1], t[0]), jnp.where(lane < 64, t[2], t[1]), t[2]]


def lists(asked):
    return asked >> LOW_BITS, asked & (LOW - 1)


def find_rows(asked, folded, picked, row_found, found_ref):
    channels = row_found.shape[0]
    highs = folded.shape[0] // channels
    high, low = lists(asked)
    span, group = 512, 32
    for chunk in range(high.shape[1] // span):
        cut = slice(span * chunk, span * (chunk + 1))
        onehot = lax.broadcasted_iota(I32, (LOW, span), 0) == low[:, cut]
        picked[...] = jnp.where(onehot, 1.0, 0.0).astype(BF16)
        row = jnp.broadcast_to(high[:, cut], (channels, span))

        def step(g, total):
            start = pl.multiple_of(g * group * channels, group * channels)
            all_high = dot(folded[pl.ds(start, group * channels), :], picked[...])
            for h in range(group):
                part = all_high[channels * h : channels * (h + 1)]
                total = total + jnp.where(row == g * group + h, part, 0.0)
            return total

        row_found[:, cut] = lax.fori_loop(
            0, highs // group, step, jnp.zeros((channels, span), F32)
        )
    for first in range(0, found_ref.shape[0], 4):
        pieces = unpacked(row_found[:, 96 * first : 96 * (first + 4)])
        for i, piece in enumerate(pieces):
            found_ref[first + i] = piece.astype(BF16)


def low_columns(asked, columns):
    high, low = lists(asked)
    for s in range(low.shape[1] // 128):
        lows = jnp.broadcast_to(low[:, 128 * s : 128 * (s + 1)], (128, 128)).astype(F32).T
        lows = jnp.concatenate([lows] * (LOW // 128), axis=1)
        onehot = lows == lax.broadcasted_iota(I32, (128, LOW), 1).astype(F32)
        columns[128 * s : 128 * (s + 1), :] = jnp.where(onehot, 1.0, 0.0).astype(BF16)


def add_rows(asked, values, columns, first, group, sums_ref):
    channels = values.shape[0]
    high, _ = lists(asked)
    row = jnp.broadcast_to(high.astype(F32).astype(BF16), values.shape)
    zero = jnp.zeros_like(values)
    rows = [jnp.where(row == jnp.asarray(first + h, BF16), values, zero) for h in range(group)]
    sums = dot(jnp.concatenate(rows, axis=0), columns[...])
    for h in range(group):
        sums_ref[:, LOW * h : LOW * (h + 1)] = sums[channels * h : channels * (h + 1)]


def step_body(
    seq, chan, filter_scale, score_scale,
    ids_ref, counts_ref, *refs,
):
    later_hbm, refs = refs[:13], refs[13:]
    *moved_hbm, half_hbm = refs[:6]
    (
    data_s, data_r, ask_s, ask_r, conv_s, conv_r, found_s, found_r, enc_s, enc_r, embed_s, embed_r,
    negs_s, negs_r, slot_s, slot_r, gback_s, gback_r, out_s, out_r, res_s, res_r,
    place, flat, pre, spec, picked_rows, folded, picked, row_found, columns, sums, places,
    send_sems, recv_sems, local_sems, out_sems, back, gate_grad, values_ref, asked_ref,
    *later,
    ) = refs[6:]
    (
        signal_ref, taps_ref, item, lanes_ref, gain_ref, fwd1, fwd2, inv2, inv1, turns,
        gate_ref, positive_ref, table,
    ) = later
    channels, length = signal_ref.shape
    units = length // 128
    own = channels // seq
    groups = place.shape[0]

    def sems(i):
        return send_sems.at[i], recv_sems.at[i]

    data_x = Exchange("seq", seq, data_s, data_r, sems(0))
    ask_x = Exchange("seq", seq, ask_s, ask_r, sems(1))
    conv_x = Exchange("seq", seq, conv_s, conv_r, sems(2))
    found_x = Exchange("seq", seq, found_s, found_r, sems(3))
    enc_x = Exchange("chan", chan, enc_s, enc_r, sems(4))
    embed_x = Exchange("chan", chan, embed_s, embed_r, sems(5))
    negs_x = Exchange("chan", chan, negs_s, negs_r, sems(6))
    slot_x = Exchange("chan", chan, slot_s, slot_r, sems(7))
    gback_x = Exchange("seq", seq, gback_s, gback_r, sems(8))
    out_x = Exchange("seq", seq, out_s, out_r, sems(9))
    res_x = Exchange("seq", seq, res_s, res_r, sems(10))

    barrier = pltpu.get_barrier_semaphore()
    for axis, size in (("seq", seq), ("chan", chan)):
        me = lax.axis_index(axis)
        for step in range(1, size):
            pl.semaphore_signal(
                barrier,
                inc=1,
                device_id={axis: lax.rem(me + step, size)},
                device_id_type=pl.DeviceIdType.MESH,
            )
    loads = [
        pltpu.make_async_copy(s, t, local_sems.at[i])
        for i, (s, t) in enumerate(zip(later_hbm, later))
    ]
    for load in loads:
        load.start()

    outs = [
        pltpu.make_async_copy(s, t, out_sems.at[i])
        for i, (s, t) in enumerate(zip((res_r, back, gate_grad, values_ref, asked_ref), moved_hbm))
    ]
    for kind, ref in enumerate((signal_ref, taps_ref)):
        loads[kind].wait()
        value = to_rows(ref[...].astype(F32), flat).astype(BF16)
        data_s[:, kind] = value.reshape(seq, own, units, 128)
    loads[2].wait()
    per = ids_ref.shape[1]

    @pl.loop(0, ids_ref.shape[0])
    def _(u):
        for j in range(per):
            picked_rows[pl.ds(u * per + j, 1), :] = item[pl.ds(ids_ref[u, j] >> 7, 1), :]

    pl.semaphore_wait(barrier, seq + chan - 2)
    data_x.start()

    rows = []
    loads[3].wait()
    ids = lanes_ref[...].astype(F32)
    lane_at = jnp.concatenate(
        [
            jnp.concatenate([ids[2 * b : 2 * b + 1], ids[2 * b + 1 : 2 * b + 2]], axis=1)
            for b in range(groups)
        ],
        axis=0,
    )
    lane_at = lane_at.astype(I32) & 127
    for b in range(groups):
        block = picked_rows[128 * b : 128 * (b + 1), :].astype(F32).T
        here = lax.broadcasted_iota(I32, (128, 128), 0) == lane_at[b : b + 1, :]
        rows.append(jnp.sum(jnp.where(here, block, 0.0), axis=0, keepdims=True))
    turned = (96 * lax.axis_index("seq")) & 127
    requests(jnp.concatenate(rows, axis=0).astype(I32), turned, ask_s, place)
    ask_x.start()

    for load in loads[4:]:
        load.wait()
    for h in range(table.shape[1] // LOW):
        folded[channels * h : channels * (h + 1), :] = table[:, LOW * h : LOW * (h + 1)]
    turn_r, turn_i = turns[:, :N2], turns[:, N2:]
    data_x.wait()
    spectra = spectrum(
        [data_r[:, kind, c].reshape(N1, N2) for kind in range(2) for c in range(own)],
        fwd1[...], fwd2[...], turn_r, turn_i,
    )
    for i, (real, imag) in enumerate(spectra):
        spec[i, 0] = real
        spec[i, 1] = imag
    products = []
    for c in range(own):
        (xr, xi), (hr, hi) = spectra[c], spectra[own + c]
        products.append((xr * hr - xi * hi, xr * hi + xi * hr))
    for c, value in enumerate(positions(products, inv2[...], inv1[...], turn_r, turn_i)):
        conv_s[:, c] = value.astype(BF16).reshape(seq, units, 128)
    conv_x.start()

    ask_x.wait()
    asked = packed([ask_r[s][0:1, :] for s in range(seq)]).astype(I32) - 1
    asked_ref[...] = jnp.broadcast_to(asked, asked_ref.shape)
    outs[4].start()
    find_rows(asked, folded, picked, row_found, found_s)
    found_x.start()

    conv_x.wait()
    flat[...] = conv_r[...].reshape(channels * units, 128).astype(F32)
    square = lax.broadcasted_iota(I32, (channels, channels), 0) == lax.broadcasted_iota(
        I32, (channels, channels), 1
    )
    gain = jnp.sum(jnp.where(square, gain_ref[...], 0.0), axis=1, keepdims=True)
    tops = []
    for u in range(units):
        cut = slice(128 * u, 128 * (u + 1))
        conv = flat[pl.ds(u, channels, stride=units), :]
        value = filter_scale * conv + gain * signal_ref[:, cut].astype(F32)
        pre[:, cut] = value
        coded = (gate_ref[:, cut].astype(F32) * value).astype(BF16)
        enc_s[u // 2, :, 128 * (u % 2) : 128 * (u % 2 + 1)] = coded
        tops.append(
            jnp.sum(coded.astype(F32) * positive_ref[:, cut].astype(F32), axis=0, keepdims=True)
        )
    enc_x.start()
    for b in range(groups):
        top = jnp.concatenate(tops[2 * b : 2 * b + 2] + [jnp.zeros((14, 128), F32)], axis=0)
        embed_s[b, channels:, :] = top.astype(BF16)
        slot = lax.broadcasted_iota(I32, (seq * 128, 128), 0)
        places[b] = jnp.where(slot == place[b : b + 1, :], 1.0, 0.0).astype(BF16)

    found_x.wait()
    found = jnp.concatenate([found_r[o] for o in range(seq)], axis=1)
    for b in range(groups):
        embed_s[b, :channels, :] = dot(found, places[b]).astype(BF16)
    embed_x.start()

    low_columns(asked_ref[0:1, :], columns)
    enc_x.wait()
    coded = jnp.concatenate([enc_r[z] for z in range(chan)], axis=0)
    line = lax.broadcasted_iota(I32, (128, 128), 0)
    mine = 2 * lax.axis_index("chan")
    limit = jnp.where(line < 64, counts_ref[mine], 64 + counts_ref[mine + 1])
    embed_x.wait()
    embed = jnp.concatenate([embed_r[z, :channels, :] for z in range(chan)], axis=0)
    score = dot(embed, coded, TN)
    score = score_scale * jnp.where(line < 64, score[:, :128], score[:, 128:])
    weight = jnp.where(line < limit, 1.0 / (1.0 + jnp.exp(-score)), 0.0)
    weight = jnp.concatenate(
        [jnp.where(line < 64, weight, 0.0), jnp.where(line < 64, 0.0, weight)], axis=1
    ).astype(BF16)
    top = embed_r[0, channels:, :].astype(F32)
    for z in range(1, chan):
        top = top + embed_r[z, channels:, :].astype(F32)
    top = -1.0 / (1.0 + jnp.exp(score_scale * top))
    negs = dot(embed, weight).astype(BF16)
    for z in range(chan):
        negs_s[z, :channels, :] = negs[channels * z : channels * (z + 1)]
        negs_s[z, channels:, :128] = top.astype(BF16)
        negs_s[z, channels:, 128:] = top.astype(BF16)
    negs_x.start()
    slot = (score_scale * dot(coded, weight, NT)).astype(BF16)
    for z in range(chan):
        slot_s[z] = slot[channels * z : channels * (z + 1)]
    slot_x.start()

    negs_x.wait()
    for u in range(units):
        b, half = divmod(u, 2)
        cut, side = slice(128 * u, 128 * (u + 1)), slice(128 * half, 128 * (half + 1))
        top = negs_r[b, channels:, side].astype(F32)[half : half + 1, :]
        positive = positive_ref[:, cut].astype(F32)
        grad = score_scale * (top * positive + negs_r[b, :channels, side].astype(F32))
        gate_grad[:, cut] = (grad * pre[:, cut]).astype(BF16)
        value = grad * gate_ref[:, cut].astype(F32)
        back[:, cut] = gain * value
        flat[pl.ds(u, channels, stride=units), :] = value
    gback_s[...] = flat[...].astype(BF16).reshape(gback_s.shape)
    gback_x.start()
    outs[1].start()
    outs[2].start()

    slot_x.wait()
    outgoing = jnp.zeros((channels, seq * 128), F32)
    for b in range(groups):
        outgoing = outgoing + dot(slot_r[b], places[b], NT)
    for o in range(seq):
        out_s[o] = outgoing[:, 128 * o : 128 * (o + 1)].astype(BF16)
    out_x.start()

    gback_x.wait()
    spectra = spectrum(
        [gback_r[:, c].reshape(N1, N2) for c in range(own)], fwd1[...], fwd2[...], turn_r, turn_i
    )
    products = []
    for kind in (1, 0):
        for c in range(own):
            (br, bi), at = spectra[c], kind * own + c
            sr, si = spec[at, 0], spec[at, 1]
            products.append((sr * br + si * bi, sr * bi - si * br))
    for i, value in enumerate(positions(products, inv2[...], inv1[...], turn_r, turn_i)):
        res_s[:, i // own, i % own] = value.astype(BF16).reshape(seq, units, 128)
    res_x.start()

    out_x.wait()
    values_ref[...] = packed([out_r[s].astype(F32) for s in range(seq)]).astype(BF16)
    outs[3].start()
    groups, _, span = sums.shape
    halves = [
        pltpu.make_async_copy(
            sums.at[g], half_hbm.at[:, span * g : span * (g + 1)], out_sems.at[len(outs) + g]
        )
        for g in range(groups)
    ]
    group = span // LOW
    for g in range(groups):
        add_rows(asked_ref[0:1, :], values_ref[...], columns, group * g, group, sums.at[g])
        halves[g].start()
    res_x.wait()
    outs[0].start()
    for copy in outs + halves:
        copy.wait()


def last_body(
    scale, lag_hbm, back_hbm, gate_hbm, values_hbm, asked_hbm, half_hbm,
    grad_signal_hbm, grad_gate_hbm, grad_filter_hbm, grad_table_hbm,
    flat, columns, held, sums, lag_ref, back_ref, gate_ref, values_ref, asked_ref, results,
    in_sems, out_sems,
):
    pieces, _, span = held.shape
    loads, copies = [], []
    for i in range(pieces):
        cut = slice(span * i, span * (i + 1))
        loads.append(pltpu.make_async_copy(half_hbm.at[:, cut], held.at[i], in_sems.at[i]))
        copies.append(
            pltpu.make_async_copy(held.at[i], grad_table_hbm.at[:, cut], out_sems.at[i])
        )
    for i in range(sums.shape[0]):
        start = span * pieces + sums.shape[2] * i
        copies.append(
            pltpu.make_async_copy(
                sums.at[i],
                grad_table_hbm.at[:, start : start + sums.shape[2]],
                out_sems.at[pieces + i],
            )
        )
    small = [
        pltpu.make_async_copy(source, target, in_sems.at[pieces + i])
        for i, (source, target) in enumerate(
            (
                (asked_hbm, asked_ref),
                (values_hbm, values_ref),
                (gate_hbm, gate_ref),
                (lag_hbm, lag_ref),
                (back_hbm, back_ref),
            )
        )
    ]
    for load in small[:2] + loads + small[2:]:
        load.start()
    ends = [
        pltpu.make_async_copy(source, target, out_sems.at[len(copies) + i])
        for i, (source, target) in enumerate(
            (
                (results.at[0], grad_signal_hbm),
                (results.at[1], grad_filter_hbm),
                (gate_ref, grad_gate_hbm),
            )
        )
    ]
    small[0].wait()
    asked = asked_ref[0:1, :]
    low_columns(asked, columns)
    for i in range(pieces):
        loads[i].wait()
        copies[i].start()
    small[1].wait()
    group = sums.shape[2] // LOW
    for i in range(sums.shape[0]):
        first = span * pieces // LOW + group * i
        add_rows(asked, values_ref[...], columns, first, group, sums.at[i])
        copies[pieces + i].start()
    for load in small[2:]:
        load.wait()
    ends[2].start()
    channels, length = back_ref.shape
    units = length // 128
    for kind in range(2):
        flat[...] = lag_ref[:, kind].reshape(channels * units, 128).astype(F32)
        for u in range(units):
            cut = slice(128 * u, 128 * (u + 1))
            value = scale * flat[pl.ds(u, channels, stride=units), :]
            results[kind, :, cut] = value + back_ref[:, cut] if kind == 0 else value
        ends[kind].start()
    for copy in copies + ends:
        copy.wait()


def local(
    seq, chan, signal, gate_values, filter_taps, skip_gain, positive, item_table, item_row,
    negative_ids, block_counts,
):
    channels, length = signal.shape
    units, own = length // 128, channels // seq
    rows_own = item_table.shape[1]
    slots = negative_ids.size
    groups = slots // 128
    first_highs = 48
    half = LOW * first_highs
    rest = rows_own - half
    tables = [jnp.asarray(t) for t in transform_tables()]
    later = [
        signal, filter_taps, item_row.reshape(-1, 128), negative_ids, skip_gain.reshape(1, channels),
        *tables, gate_values, positive, item_table,
    ]
    seq_pair = lambda *shape: [pltpu.VMEM((seq, *shape), BF16)] * 2
    scratch = [
        *seq_pair(2, own, units, 128),
        *[pltpu.VMEM((seq, 8, 128), F32)] * 2,
        *seq_pair(own, units, 128),
        *seq_pair(channels, 128),
        *[pltpu.VMEM((chan, channels, 256), BF16)] * 2,
        *[pltpu.VMEM((chan, channels + 16, 128), BF16)] * 2,
        *[pltpu.VMEM((chan, channels + 16, 256), BF16)] * 2,
        *[pltpu.VMEM((chan, channels, 128), BF16)] * 2,
        *seq_pair(own, units, 128),
        *seq_pair(channels, 128),
        *seq_pair(2, own, units, 128),
        pltpu.VMEM((groups, 128), I32),
        pltpu.VMEM((channels * units, 128), F32),
        pltpu.VMEM((channels, length), F32),
        pltpu.VMEM((2 * own, 2, N1, N2), F32),
        pltpu.VMEM((slots, 128), I32),
        pltpu.VMEM((channels * rows_own // LOW, LOW), BF16),
        pltpu.VMEM((LOW, 512), BF16),
        pltpu.VMEM((channels, seq * 96), F32),
        pltpu.VMEM((seq * 96, LOW), BF16),
        pltpu.VMEM((3, channels, half // 3), F32),
        pltpu.VMEM((groups, seq * 128, 128), BF16),
        pltpu.SemaphoreType.DMA((11,)),
        pltpu.SemaphoreType.DMA((11,)),
        pltpu.SemaphoreType.DMA((len(later),)),
        pltpu.SemaphoreType.DMA((8,)),
        pltpu.VMEM((channels, length), F32),
        pltpu.VMEM((channels, length), BF16),
        pltpu.VMEM((channels, seq * 96), BF16),
        pltpu.VMEM((8, seq * 96), I32),
        *[pltpu.VMEM(a.shape, a.dtype) for a in later],
    ]
    moved = pl.pallas_call(
        functools.partial(step_body, seq, chan, (seq * length) ** -0.5, C**-0.5),
        out_shape=[
            jax.ShapeDtypeStruct((seq, 2, own, units, 128), BF16),
            jax.ShapeDtypeStruct((channels, length), F32),
            jax.ShapeDtypeStruct((channels, length), BF16),
            jax.ShapeDtypeStruct((channels, seq * 96), BF16),
            jax.ShapeDtypeStruct((8, seq * 96), I32),
            jax.ShapeDtypeStruct((channels, half), F32),
        ],
        in_specs=[SMEM] * 2 + [ANY] * len(later),
        out_specs=[ANY] * 6,
        scratch_shapes=scratch,
        compiler_params=pltpu.CompilerParams(
            collective_id=1, has_side_effects=True, vmem_limit_bytes=LIMIT
        ),
        name="step",
    )(negative_ids, block_counts, *later)
    return pl.pallas_call(
        functools.partial(last_body, (seq * length) ** -0.5),
        out_shape=[
            jax.ShapeDtypeStruct((channels, length), F32),
            jax.ShapeDtypeStruct((channels, length), BF16),
            jax.ShapeDtypeStruct((channels, length), F32),
            jax.ShapeDtypeStruct((channels, rows_own), F32),
        ],
        in_specs=[ANY] * 6,
        out_specs=[ANY] * 4,
        scratch_shapes=[
            pltpu.VMEM((channels * units, 128), F32),
            pltpu.VMEM((seq * 96, LOW), BF16),
            pltpu.VMEM((4, channels, half // 4), F32),
            pltpu.VMEM((2, channels, rest // 2), F32),
            pltpu.VMEM((seq, 2, own, units, 128), BF16),
            pltpu.VMEM((channels, length), F32),
            pltpu.VMEM((channels, length), BF16),
            pltpu.VMEM((channels, seq * 96), BF16),
            pltpu.VMEM((8, seq * 96), I32),
            pltpu.VMEM((2, channels, length), F32),
            pltpu.SemaphoreType.DMA((9,)),
            pltpu.SemaphoreType.DMA((9,)),
        ],
        compiler_params=pltpu.CompilerParams(vmem_limit_bytes=LIMIT),
        name="last",
    )(*moved)


def solution(mesh):
    in_specs = (
        P("chan", "seq"),
        P("chan", "seq"),
        P("chan", "seq"),
        P("chan"),
        P("chan", "seq"),
        P("chan", "seq"),
        P(),
        P("seq", None),
        P("seq"),
    )
    out_specs = (P("chan", "seq"),) * 4
    body = functools.partial(local, mesh.shape["seq"], mesh.shape["chan"])
    return jax.shard_map(body, mesh=mesh, in_specs=in_specs, out_specs=out_specs, check_vma=False)
```
